32 devices in a mesh: ctx: 16 (over z, x, core), vocab: 2 (over y).
Axes of the slice: x: 2, y: 2, z: 4, core: 2. Of those that a mesh axis runs over, the one named last changes fastest.
Arguments:
- hidden: bfloat16 [4096, 8192], P('ctx', 'vocab'), may hold values from -540 to 540
- norm_gain: float32 [8192], P('vocab'), may hold values from 0.5 to 1.5
- head: bfloat16 [15808, 8192], P('ctx', 'vocab'), may hold values from -0.53033009 to 0.53033009
- masked_pos: int32 [2, 16], replicated, may hold values from 0 to 2047, as said below
- masked_targets: int32 [2, 16], replicated, may hold values from 0 to 15807
- t_num: int32 [2], replicated, may hold values from 1 to 3, as said below
- t_den: int32 [2], replicated, may hold values from 192 to 319
Outputs:
- loss_value: float32 [], replicated
- grad_hidden: bfloat16 [4096, 8192], P('ctx', 'vocab')
- grad_head: bfloat16 [15808, 8192], P('ctx', 'vocab')
- grad_gain: float32 [8192], P('vocab')
The draws below stay inside these ranges and needn't reach their ends.
Inputs may be any that keep to these rules, and one draw needn't show every extreme that they name: `masked_pos`: each row lists 16 distinct positions of one sequence in increasing order; at most 8 of them fall in one aligned block of 256 positions, and exactly 8 in some blocks of every sequence. `t_num`: the two numerators differ.
All inputs are finite; a program needn't handle non-finite values.
Results may differ from the reference program's by a relative error of at most 0.0081.
Values may be sent and summed in bfloat16 or wider, within the bound.
No kernel may reach another device: no remote copies, remote signals or barrier semaphores. Data moves between devices by JAX's collectives and lax.ppermute only.
A program may use at most 64 MiB of HBM per device.

```python
import math
import jax
import jax.numpy as jnp
import numpy as np
from jax import lax

D = 8192
TOK_DEV = 256
CAP = 8
VOC = 15808
TOKENS = 4096
LENGTH = 2048
KSEQ = 16


def loud_factor():
    return max(2.0, 80.0 / math.sqrt(D))


def loud_table(key):
    loud_count = max(VOC // 16, 2)
    order = jax.random.permutation(jax.random.fold_in(key, 13), VOC)
    is_loud = order < loud_count
    loud_list = jnp.argsort(order)[:loud_count].astype(jnp.int32)
    return (is_loud, loud_list)


def head_rows(key, row_ids):
    base_key = jax.random.fold_in(key, 11)
    is_loud, loud_list = loud_table(key)

    def draw_row(row_index):
        return jnp.clip(jax.random.normal(jax.random.fold_in(base_key, row_index), (D,), jnp.float32), -6.0, 6.0)
    scale_rows = jnp.where(is_loud[row_ids], loud_factor(), 1.0)[:, None]
    return jax.vmap(draw_row)(row_ids) * scale_rows * (4.0 / math.sqrt(D))


def draw_head(key, part):
    return head_rows(key, jnp.arange(VOC, dtype=jnp.int32)).astype(jnp.bfloat16)


def draw_t_num(key, part):
    num_key = jax.random.fold_in(key, 41)
    first_key, step_key = jax.random.split(num_key, 2)
    first = jax.random.randint(first_key, (), 1, 4)
    second = (first - 1 + jax.random.randint(step_key, (), 1, 3)) % 3 + 1
    return jnp.stack([first, second]).astype(jnp.int32)


def draw_hidden(key, part):
    hidden_key = jax.random.fold_in(key, 23)
    row_key = jax.random.fold_in(hidden_key, 0)
    col_key = jax.random.fold_in(hidden_key, 1)
    main_key = jax.random.fold_in(hidden_key, 2)
    pick_key = jax.random.fold_in(hidden_key, 4)
    mix_key = jax.random.fold_in(hidden_key, 5)
    gap_key = jax.random.fold_in(hidden_key, 6)
    amp_key = jax.random.fold_in(hidden_key, 7)
    row_amp = jnp.exp(jax.random.uniform(row_key, (TOKENS, 1), jnp.float32) * math.log(10.0))
    rising = jnp.exp(jnp.arange(D, dtype=jnp.float32) * (0.5 * math.log(3.0) / D))
    col_amp = jnp.exp(jax.random.uniform(col_key, (1, D), jnp.float32) * math.log(10.0)) * rising[None, :]
    values = jnp.clip(jax.random.normal(main_key, (TOKENS, D), jnp.float32), -3.0, 3.0) * row_amp * col_amp
    is_loud, loud_list = loud_table(key)
    loud_count = loud_list.shape[0]
    aligned = jnp.arange(0, TOKENS, 3, dtype=jnp.int32)
    count_aligned = aligned.shape[0]
    first_key, second_key, third_key = jax.random.split(pick_key, 3)
    first_slot = jax.random.randint(first_key, (count_aligned,), 0, loud_count)
    second_slot = (first_slot + jax.random.randint(second_key, (count_aligned,), 1, loud_count)) % loud_count
    third_slot = (first_slot + jax.random.randint(third_key, (count_aligned,), 1, loud_count)) % loud_count
    first = head_rows(key, loud_list[first_slot])
    second = head_rows(key, loud_list[second_slot])
    third = head_rows(key, loud_list[third_slot])
    mixing = jax.random.uniform(mix_key, (count_aligned, 1), jnp.float32)
    base_mix = first + second + mixing * third
    score_gap = jax.random.uniform(gap_key, (count_aligned,), jnp.float32, 1.5, 2.5)
    length_mix = jnp.sqrt(jnp.sum(base_mix * base_mix, axis=1))
    diff_mix = jnp.sum(base_mix * (first - second), axis=1)
    denominator = jnp.sum(first * (first - second), axis=1)
    along_first = (score_gap * length_mix / math.sqrt(D) - diff_mix) / denominator
    amplitude = jnp.exp(jax.random.uniform(amp_key, (count_aligned, 1), jnp.float32) * math.log(10.0))
    mixed_rows = (base_mix + along_first[:, None] * first) * (amplitude / loud_factor())
    values = values.at[aligned].set(mixed_rows)
    return values.astype(jnp.bfloat16)


def draw_one_sequence(seq_key):
    blocks = LENGTH // TOK_DEV
    hot_count = blocks // 8
    order_key, slot_key, place_key = jax.random.split(seq_key, 3)
    block_order = jax.random.permutation(order_key, blocks)
    is_hot = jnp.zeros((blocks,), jnp.bool_).at[block_order[:hot_count]].set(True)
    slot_score = jax.random.permutation(slot_key, blocks * CAP).reshape(blocks, CAP)
    slot_score = jnp.where(is_hot[:, None], slot_score + blocks * CAP, slot_score)
    slot_rank = jnp.argsort(jnp.argsort(slot_score.reshape(-1))).reshape(blocks, CAP)
    chosen = (slot_rank < KSEQ - hot_count * CAP).astype(jnp.int32)
    counts = jnp.where(is_hot, CAP, jnp.sum(chosen, axis=1))
    place_keys = jax.random.split(place_key, blocks)

    def block_places(block_key):
        return jax.random.permutation(block_key, TOK_DEV)
    places = jax.vmap(block_places)(place_keys)
    selected = (places < counts[:, None]).reshape(-1)
    return jnp.nonzero(selected, size=KSEQ)[0].astype(jnp.int32)


def draw_masked_pos(key, part):
    seq_keys = jax.random.split(jax.random.fold_in(key, 37), 2)
    return jax.vmap(draw_one_sequence)(seq_keys)


def touch_ends(result, key, low, largest):
    spot = [jax.random.randint(jax.random.fold_in(key, axis), (), 0, length) for axis, length in enumerate(result.shape)]
    main_axis = result.shape.index(max(result.shape))
    beside = spot[:main_axis] + [(spot[main_axis] + 1) % result.shape[main_axis]] + spot[main_axis + 1:]
    return result.at[tuple(spot)].set(low).at[tuple(beside)].set(largest)


def rank_bounds(amount, slope):
    weights = [(1 << 20) // math.isqrt(rank ** slope) + 1 for rank in range(1, amount + 1)]
    deviation = 1 + sum(weights) // (1 << 30)
    return np.cumsum(np.array([max(1, weight // deviation) for weight in weights]))


def skewed_ids(stream_key, extent, amount, slope):
    table = rank_bounds(amount, slope)
    pick = jax.random.randint(jax.random.fold_in(stream_key, 1), extent, 0, int(table[amount - 1]))
    grade = jnp.searchsorted(jnp.asarray(table, jnp.int32), pick, side="right")
    return jax.random.permutation(jax.random.fold_in(stream_key, 2), amount)[grade].astype(jnp.int32)


def setup_inputs(seed: int = 0) -> dict:
    splits = jax.random.split(jax.random.key(seed), 8)
    return {
        "hidden": draw_hidden(jax.random.fold_in(splits[7], 71), 0),
        "norm_gain": jnp.clip(1.0 + 0.1 * jax.random.normal(splits[1], (D,), jnp.float32), 0.5, 1.5),
        "head": draw_head(jax.random.fold_in(splits[7], 71), 0),
        "masked_pos": draw_masked_pos(jax.random.fold_in(splits[7], 71), 0),
        "masked_targets": touch_ends(skewed_ids(splits[4], (2, KSEQ), VOC, 2), jax.random.fold_in(splits[4], 3), 0, VOC - 1).astype(jnp.int32),
        "t_num": draw_t_num(jax.random.fold_in(splits[7], 71), 0),
        "t_den": jax.random.randint(splits[6], (2,), 192, 320).astype(jnp.int32),
    }


EPSILON = 1e-05
LOSS_SCALE = 1024.0

def reference(hidden, norm_gain, head, masked_pos, masked_targets, t_num, t_den):
    seq_base = (jnp.arange(2, dtype=jnp.int32) * LENGTH)[:, None]
    where_rows = (masked_pos + seq_base).reshape(-1).astype(jnp.int32)
    masked_rows = hidden[where_rows].astype(jnp.float32)
    inverse = lax.rsqrt(lax.optimization_barrier(jnp.mean(masked_rows * masked_rows, axis=1)) + EPSILON)
    normed = (masked_rows * inverse[:, None] * norm_gain[None, :]).astype(jnp.bfloat16)
    logits = lax.dot_general(normed, head, (((1,), (1,)), ((), ())), preferred_element_type=jnp.float32)
    row_top = lax.optimization_barrier(jnp.max(logits, axis=1, keepdims=True))
    exp_total = lax.optimization_barrier(jnp.sum(jnp.exp(logits - row_top), axis=1))
    log_total = row_top[:, 0] + jnp.log(exp_total)
    targets = masked_targets.reshape(-1).astype(jnp.int32)
    picked = jnp.take_along_axis(logits, targets[:, None], axis=1)[:, 0]
    weight = t_den.astype(jnp.float32) / (t_num.astype(jnp.float32) * (2.0 * LENGTH))
    factor = jnp.repeat(weight, KSEQ)
    loss_value = jnp.sum(factor * (log_total - picked))
    softmax_out = jnp.exp(logits - log_total[:, None])
    onehot = (jnp.arange(logits.shape[1], dtype=jnp.int32)[None, :] == targets[:, None]).astype(jnp.float32)
    dlogits = ((LOSS_SCALE * factor)[:, None] * (softmax_out - onehot)).astype(jnp.bfloat16)
    grad_head = lax.dot_general(dlogits, normed, (((0,), (0,)), ((), ())), preferred_element_type=jnp.float32).astype(jnp.bfloat16)
    dnormed = jnp.dot(dlogits, head, preferred_element_type=jnp.float32)
    grad_gain = lax.optimization_barrier(jnp.sum(dnormed * masked_rows * inverse[:, None], axis=0))
    inner_mean = lax.optimization_barrier(jnp.mean(norm_gain[None, :] * dnormed * masked_rows, axis=1))
    row_grads = inverse[:, None] * norm_gain[None, :] * dnormed - masked_rows * (inverse * inverse * inverse * inner_mean)[:, None]
    grad_hidden = jnp.zeros(hidden.shape, jnp.bfloat16).at[where_rows].set(row_grads.astype(jnp.bfloat16))
    return (loss_value, grad_hidden, grad_head, grad_gain)
```

```python
import jax
import jax.numpy as jnp
from jax import lax
from jax.sharding import PartitionSpec as P

EPSILON = 1e-05
LOSS_SCALE = 1024.0
LANES = 128
F32 = jnp.float32
BF16 = jnp.bfloat16


def swap(x, axis, bit):
    return lax.ppermute(x, axis, [(i, i ^ bit) for i in range(lax.axis_size(axis))])


def sum_over(x, axis):
    bit = 1
    while bit < lax.axis_size(axis):
        x = x + swap(x, axis, bit)
        bit *= 2
    return x


def three_parts(x):
    high = x.astype(BF16)
    rest = x - high.astype(F32)
    middle = rest.astype(BF16)
    low = (rest - middle.astype(F32)).astype(BF16)
    return [high, middle, low]


def on_device(hidden, norm_gain, head, masked_pos, masked_targets, t_num, t_den):
    tok_here, width_here = hidden.shape
    voc_here = head.shape[0]
    ctx_count = lax.axis_size("ctx")
    model_width = width_here * lax.axis_size("vocab")
    ctx_index = lax.axis_index("ctx")
    blocks = ctx_count // 2
    slots = masked_pos.shape[1]
    half = width_here // 2
    seq_here = ctx_index // blocks
    block_here = ctx_index % blocks
    core = ctx_index % 2
    inner_bits = [1 << b for b in range(1, ctx_count.bit_length() - 2)]

    def own_half(x, other=False):
        start = (1 - core if other else core) * half
        return lax.dynamic_slice_in_dim(x, start, half, 1)

    def by_core(mine, theirs):
        first = jnp.where(core == 0, mine, theirs)
        second = jnp.where(core == 0, theirs, mine)
        return first, second

    local_pos = masked_pos[seq_here] - block_here * tok_here
    select = (
        jnp.arange(tok_here, dtype=jnp.int32)[None, :] == local_pos[:, None]
    ).astype(BF16)
    own = jnp.dot(select, hidden, preferred_element_type=F32)
    squares = sum_over(jnp.sum(own * own, axis=1), "vocab")
    own16 = own.astype(BF16)
    tail = jnp.concatenate(
        [p[:, None] for p in three_parts(squares)] + [jnp.zeros((slots, LANES - 3), BF16)], axis=1
    )
    packed = jnp.concatenate([own_half(own16), tail], axis=1) + swap(
        jnp.concatenate([own_half(own16, True), tail], axis=1), "ctx", 1
    )
    for bit in inner_bits:
        packed = packed + swap(packed, "ctx", bit)
    there = swap(packed, "ctx", blocks)
    both = jnp.where(
        seq_here == 0,
        jnp.concatenate([packed, there], axis=0),
        jnp.concatenate([there, packed], axis=0),
    )
    first, second = by_core(both[:, :half], swap(both[:, :half], "ctx", 1))
    rows = jnp.concatenate([first, second], axis=1).astype(F32)
    square_sum = jnp.sum(both[:, half : half + 3].astype(F32), axis=1)
    inverse = lax.rsqrt(square_sum / model_width + EPSILON)
    normed = (rows * inverse[:, None] * norm_gain[None, :]).astype(BF16)

    logits = lax.dot_general(
        normed, head, (((1,), (1,)), ((), ())), preferred_element_type=F32
    )
    logits = sum_over(logits, "vocab")

    row_total = 2 * slots
    targets = masked_targets.reshape(-1) - ctx_index * voc_here
    is_target = jnp.arange(voc_here, dtype=jnp.int32)[None, :] == targets[:, None]
    top = jnp.max(logits, axis=1)
    away = logits - top[:, None]
    exps = jnp.exp(away)
    stats = jnp.concatenate(
        [
            top,
            jnp.sum(exps, axis=1),
            jnp.sum(exps * away, axis=1),
            jnp.sum(jnp.where(is_target, logits, 0.0), axis=1),
        ]
    )
    slot = jnp.arange(ctx_count, dtype=jnp.int32) == ctx_index
    table = jnp.where(slot[:, None], stats[None], 0.0)
    bit = 1
    while bit < ctx_count:
        table = table + swap(table, "ctx", bit)
        bit *= 2
    table = table.reshape(ctx_count, 4, row_total)
    row_top = jnp.max(table[:, 0], axis=0)
    weights = jnp.exp(table[:, 0] - row_top[None])
    exp_total = jnp.sum(table[:, 1] * weights, axis=0)
    moment = jnp.sum(weights * (table[:, 2] + (table[:, 0] - row_top[None]) * table[:, 1]), axis=0)
    picked = jnp.sum(table[:, 3], axis=0)
    log_total = row_top + jnp.log(exp_total)
    weight = t_den.astype(F32) / (t_num.astype(F32) * (2.0 * tok_here * blocks))
    factor = jnp.repeat(weight, slots, total_repeat_length=row_total)
    loss_value = jnp.sum(factor * (log_total - picked))
    scale = LOSS_SCALE * factor
    inner_mean = scale * (moment / exp_total - (picked - row_top)) / inverse / model_width

    dlogits = (
        scale[:, None] * (jnp.exp(logits - log_total[:, None]) - is_target.astype(F32))
    ).astype(BF16)
    part = jnp.dot(dlogits, head, preferred_element_type=F32)
    gain_part = jnp.sum(part * rows * inverse[:, None], axis=0, keepdims=True)

    def packed_gain(x):
        return x.reshape(slots, half // slots).astype(BF16)

    send = jnp.concatenate([own_half(part, True).astype(BF16).reshape(2, slots, half)], axis=0)
    mine = own_half(part).reshape(2, slots, half)
    gain_mine = packed_gain(own_half(gain_part)).astype(F32)
    gain_send = packed_gain(own_half(gain_part, True))
    arrived = swap(jnp.concatenate([send[0], send[1], gain_send], axis=1), "ctx", 1).astype(F32)
    mine = mine + jnp.stack([arrived[:, :half], arrived[:, half : 2 * half]])
    gain_mine = (gain_mine + arrived[:, 2 * half :]).astype(BF16)
    keep = jnp.where(seq_here == 0, mine[0], mine[1])
    give = jnp.where(seq_here == 0, mine[1], mine[0]).astype(BF16)
    arrived = swap(jnp.concatenate([give, gain_mine], axis=1), "ctx", blocks).astype(F32)
    total = jnp.concatenate([keep, gain_mine.astype(F32)], axis=1) + arrived
    for bit in inner_bits:
        sent = total.astype(BF16)
        total = sent.astype(F32) + swap(sent, "ctx", bit).astype(F32)
    sent = total.astype(BF16)
    other = swap(sent, "ctx", 1)
    first, second = by_core(sent.astype(F32), other.astype(F32))
    dnormed = jnp.concatenate([first[:, :half], second[:, :half]], axis=1)
    grad_gain = jnp.concatenate([first[:, half:].reshape(-1), second[:, half:].reshape(-1)])

    grad_head = lax.dot_general(
        dlogits, normed, (((0,), (0,)), ((), ())), preferred_element_type=F32
    ).astype(BF16)

    inv_own = jnp.where(seq_here == 0, inverse[:slots], inverse[slots:])[:, None]
    mean_own = jnp.where(seq_here == 0, inner_mean[:slots], inner_mean[slots:])[:, None]
    row_grads = (
        inv_own * norm_gain[None, :] * dnormed - own * (inv_own * inv_own * inv_own * mean_own)
    ).astype(BF16)
    grad_hidden = lax.dot_general(
        select, row_grads, (((0,), (0,)), ((), ())), preferred_element_type=F32
    ).astype(BF16)
    return (loss_value, grad_hidden, grad_head, grad_gain)


def solution(mesh):
    placed = (P("ctx", "vocab"), P("vocab"), P("ctx", "vocab"), P(), P(), P(), P())
    return jax.shard_map(
        on_device,
        mesh=mesh,
        in_specs=placed,
        out_specs=(P(), P("ctx", "vocab"), P("ctx", "vocab"), P("vocab")),
        check_vma=False,
    )
```

```python
import jax
import jax.numpy as jnp
from jax import lax
from jax.experimental import pallas as pl
from jax.experimental.pallas import tpu as pltpu
from jax.sharding import PartitionSpec as P


EPSILON = 1e-05
LOSS_SCALE = 1024.0
LANES = 128
SUBLANES = 8
MIB = 1 << 20
F32 = jnp.float32
BF16 = jnp.bfloat16


def vmem():
    return pl.BlockSpec(memory_space=pltpu.VMEM)


def smem():
    return pl.BlockSpec(memory_space=pltpu.SMEM)


def anywhere():
    return pl.BlockSpec(memory_space=pl.ANY)


def params(mib):
    return pltpu.CompilerParams(vmem_limit_bytes=mib * MIB)


def cost(bytes_accessed):
    return pl.CostEstimate(flops=0, bytes_accessed=bytes_accessed, transcendentals=0)


def shape(dims, dtype):
    return jax.ShapeDtypeStruct(dims, dtype)


def swap(x, axis, bit):
    return lax.ppermute(x, axis, [(i, i ^ bit) for i in range(lax.axis_size(axis))])


def sum_over(x, axis):
    bit = 1
    while bit < lax.axis_size(axis):
        x = x + swap(x, axis, bit)
        bit *= 2
    return x


def here(blocks):
    ctx = lax.axis_index("ctx")
    return ctx, ctx // blocks, ctx % blocks, ctx % 2


def pick_kernel(select_ref, hidden_ref, own_ref, keep_ref, send_ref):
    slots, width = own_ref.shape
    half = width // 2
    core = lax.axis_index("ctx") % 2
    own = jnp.dot(select_ref[...], hidden_ref[...], preferred_element_type=F32)
    squares = jnp.sum(own * own, axis=1, keepdims=True)
    high = squares.astype(BF16).astype(F32)
    middle = (squares - high).astype(BF16).astype(F32)
    low = squares - high - middle
    lane = lax.broadcasted_iota(jnp.int32, (slots, LANES), 1)
    tail = jnp.where(lane == 0, high, jnp.where(lane == 1, middle, jnp.where(lane == 2, low, 0.0)))
    own = own.astype(BF16)
    own_ref[...] = own
    keep_ref[:, half:] = tail.astype(BF16)
    send_ref[:, half:] = tail.astype(BF16)

    @pl.when(core == 0)
    def _():
        keep_ref[:, :half] = own[:, :half]
        send_ref[:, :half] = own[:, half:]

    @pl.when(core == 1)
    def _():
        keep_ref[:, :half] = own[:, half:]
        send_ref[:, :half] = own[:, :half]


def add_kernel(first_ref, second_ref, out_ref):
    out_ref[...] = first_ref[...] + second_ref[...]


def load_kernel(start, head_ref, dep_ref, out_ref, sem):
    del dep_ref
    copy = pltpu.make_async_copy(head_ref.at[:, pl.ds(start, out_ref.shape[1])], out_ref, sem)
    copy.start()
    copy.wait()


def normalize_kernel(
    blocks, model_width, mine_ref, mine_other_ref, there_ref, there_other_ref, squares_ref,
    there_squares_ref, gain_ref, left_ref, right_ref, scaled_ref, inverse_ref,
):
    slots = mine_ref.shape[0]
    half = mine_ref.shape[1] - LANES
    _, seq, _, core = here(blocks)
    for a_ref, b_ref, s_ref, s in (
        (mine_ref, mine_other_ref, squares_ref, seq),
        (there_ref, there_other_ref, there_squares_ref, 1 - seq),
    ):
        rows = pl.ds(pl.multiple_of(s * slots, slots), slots)
        inverse = lax.rsqrt(s_ref[...] / model_width + EPSILON)
        inverse_ref[rows, :] = inverse
        inverse = inverse[:, :1]
        a = a_ref[:, :half].astype(F32)
        b = b_ref[:, :half].astype(F32)
        for part, part_ref, start in (
            (jnp.where(core == 0, a, b), left_ref, 0),
            (jnp.where(core == 0, b, a), right_ref, half),
        ):
            scaled = part * inverse
            scaled_ref[rows, start : start + half] = scaled
            part_ref[rows, :] = (scaled * gain_ref[:, start : start + half]).astype(BF16)


def targets_kernel(voc, ref, dep_ref, out_ref):
    del dep_ref
    total = out_ref.shape[0]
    slots = total // 2
    place = lax.broadcasted_iota(jnp.int32, out_ref.shape, 0)
    out = jnp.zeros(out_ref.shape, jnp.int32)
    for r in range(total):
        out = jnp.where(place == r, ref[r // slots, r % slots], out)
    out_ref[...] = out - lax.axis_index("ctx") * voc


def stats_kernel(targets_ref, first_ref, second_ref, logits_ref, exps_ref, table_ref):
    total, voc = first_ref.shape
    logits = first_ref[...] + second_ref[...]
    logits_ref[...] = logits
    is_target = lax.broadcasted_iota(jnp.int32, (total, voc), 1) == targets_ref[:, 0:1]
    top = jnp.max(logits, axis=1, keepdims=True)
    away = logits - top
    exps = jnp.exp(away)
    exps_ref[:total, :] = jnp.where(is_target, 0.0, exps).astype(BF16)
    exps_ref[total:, :] = jnp.where(is_target, 1.0, 0.0).astype(BF16)
    entries = (
        top,
        jnp.sum(exps, axis=1, keepdims=True),
        jnp.sum(exps * away, axis=1, keepdims=True),
        jnp.sum(jnp.where(is_target, logits, 0.0), axis=1, keepdims=True),
    )
    lane = lax.broadcasted_iota(jnp.int32, (LANES, LANES), 1)
    table = jnp.zeros((LANES, LANES), F32)
    for k, entry in enumerate(entries):
        entry = jnp.concatenate([entry, jnp.zeros((LANES - total, 1), F32)]) if total < LANES else entry
        table = jnp.where(lane == k, entry, table)
    table_ref[...] = table.T[:SUBLANES, :]


def merged(first, second):
    top = jnp.maximum(first[0:1], second[0:1])
    gap_first = first[0:1] - top
    gap_second = second[0:1] - top
    exp_first = jnp.exp(gap_first)
    exp_second = jnp.exp(gap_second)
    return (
        top,
        first[1:2] * exp_first + second[1:2] * exp_second,
        (first[2:3] + gap_first * first[1:2]) * exp_first
        + (second[2:3] + gap_second * second[1:2]) * exp_second,
        first[3:4] + second[3:4],
    )


def merge_kernel(first_ref, second_ref, out_ref):
    out_ref[...] = jnp.zeros_like(out_ref)
    for k, row in enumerate(merged(first_ref, second_ref)):
        out_ref[k : k + 1, :] = row


def combine_kernel(
    length, model_width, num_ref, den_ref, own_ref, a_ref, b_ref, part_left_ref, part_right_ref,
    scaled_ref, inverse_ref, keep_ref, send_ref, meta_ref, loss_ref, tail_ref, near_ref,
):
    total = inverse_ref.shape[0]
    slots = total // 2
    half = part_left_ref.shape[1]
    core = lax.axis_index("ctx") % 2
    row_top, exp_total, moment, picked = merged(a_ref, b_ref)
    log_total = row_top + jnp.log(exp_total)
    place = lax.broadcasted_iota(jnp.int32, (1, LANES), 1)
    den = jnp.where(place < slots, den_ref[0], den_ref[1]).astype(F32)
    num = jnp.where(place < slots, num_ref[0], num_ref[1]).astype(F32)
    factor = den / (num * (2.0 * length))
    loss_ref[...] = jnp.sum(
        jnp.where(place < total, factor * (log_total - picked), 0.0), axis=1, keepdims=True
    )
    scale = LOSS_SCALE * factor
    inner = scale * (moment / exp_total - (picked - row_top)) / model_width
    spread = scale * jnp.exp(own_ref[0:1, :] - log_total)
    at_target = scale * (jnp.exp(picked - log_total) - 1.0)
    near_ref[...] = jnp.zeros_like(near_ref)
    for k, row in enumerate((log_total, scale, inner, spread, at_target)):
        near_ref[k : k + 1, :] = row
    across = jnp.concatenate([near_ref[...], jnp.zeros((LANES - SUBLANES, LANES), F32)]).T[:total]
    lane = lax.broadcasted_iota(jnp.int32, (total, LANES), 1)
    meta_ref[...] = jnp.where(lane == 2, across / inverse_ref[...], across)
    spread = across[:, 3:4]
    at_target = across[:, 4:5]
    for side, part_ref in enumerate((part_left_ref, part_right_ref)):
        columns = slice(side * half, (side + 1) * half)
        part = spread * part_ref[:total, :] + at_target * part_ref[total:, :]
        gain = jnp.sum(part * scaled_ref[:, columns], axis=0, keepdims=True)
        tail_ref[...] = jnp.zeros_like(tail_ref)
        for j in range(half // LANES):
            tail_ref[j : j + 1, :] = gain[:, j * LANES : (j + 1) * LANES]

        @pl.when(core == side)
        def _():
            keep_ref[:, :half] = part
            keep_ref[:, half:] = tail_ref[...]

        @pl.when(core != side)
        def _():
            send_ref[:, :half] = part.astype(BF16)
            send_ref[:, half:] = tail_ref[...].astype(BF16)


def divide_kernel(blocks, keep_ref, arrived_ref, own_ref, give_ref):
    slots = own_ref.shape[0]
    half = own_ref.shape[1] - LANES
    _, seq, _, _ = here(blocks)
    tail = (keep_ref[:slots, half:] + arrived_ref[:slots, half:].astype(F32)).astype(BF16)
    for ref, s in ((own_ref, seq), (give_ref, 1 - seq)):
        rows = pl.ds(pl.multiple_of(s * slots, slots), slots)
        part = keep_ref[rows, :half] + arrived_ref[rows, :half].astype(F32)
        ref[:, :half] = part.astype(ref.dtype)
        ref[:, half:] = tail.astype(ref.dtype)


def dlogits_kernel(targets_ref, logits_ref, meta_ref, dep_ref, out_ref):
    del dep_ref
    total, voc = logits_ref.shape
    is_target = lax.broadcasted_iota(jnp.int32, (total, voc), 1) == targets_ref[:, 0:1]
    softmax = jnp.exp(logits_ref[...] - meta_ref[:, 0:1])
    out_ref[...] = (
        (meta_ref[:, 1:2] * (softmax - jnp.where(is_target, 1.0, 0.0))).T.astype(BF16)
    )


def head_kernel(dlogits_ref, normed_ref, *rest):
    rest[-1][...] = jnp.dot(
        dlogits_ref[...], normed_ref[...], preferred_element_type=F32
    ).astype(BF16)


def final_kernel(
    blocks, select_ref, mine_ref, other_ref, own_ref, inverse_ref, meta_ref, gain_ref, out_ref,
    grad_gain_ref, block_ref, sems,
):
    chunks, _, step = block_ref.shape
    slots = mine_ref.shape[0]
    half = mine_ref.shape[1] - LANES
    _, seq, _, core = here(blocks)
    rows = pl.ds(pl.multiple_of(seq * slots, slots), slots)
    inverse = inverse_ref[rows, :][:, :1]
    pull = inverse * inverse * inverse * meta_ref[rows, :][:, 2:3]
    copies = []
    for chunk in range(chunks):
        start = chunk * step
        columns = slice(start, start + step)
        inner = slice(start % half, start % half + step)
        dnormed = jnp.where(
            core == start // half,
            mine_ref[:, inner].astype(F32),
            other_ref[:, inner].astype(F32),
        )
        grads = inverse * gain_ref[:, columns] * dnormed - own_ref[:, columns].astype(F32) * pull
        block_ref[chunk] = lax.dot_general(
            select_ref[...],
            grads.astype(BF16),
            (((0,), (0,)), ((), ())),
            preferred_element_type=F32,
        ).astype(BF16)
        copies.append(
            pltpu.make_async_copy(block_ref.at[chunk], out_ref.at[:, columns], sems.at[chunk])
        )
        copies[-1].start()
    a = mine_ref[:, half:].astype(F32)
    b = other_ref[:, half:].astype(F32)
    for start, tail in ((0, jnp.where(core == 0, a, b)), (half, jnp.where(core == 0, b, a))):
        for j in range(half // LANES):
            grad_gain_ref[:, start + j * LANES : start + (j + 1) * LANES] = tail[j : j + 1, :]
    for copy in copies:
        copy.wait()


def device_step(hidden, norm_gain, head, masked_pos, masked_targets, t_num, t_den):
    tok, width = hidden.shape
    voc = head.shape[0]
    count = lax.axis_size("ctx")
    model_width = width * lax.axis_size("vocab")
    blocks = count // 2
    slots = masked_pos.shape[1]
    total = 2 * slots
    half = width // 2
    packed_width = half + LANES
    inner_bits = [1 << b for b in range(1, count.bit_length() - 2)]
    gain_row = norm_gain.reshape(1, width)

    ctx = lax.axis_index("ctx")
    local = masked_pos[ctx // blocks] - ctx % blocks * tok
    select = (jnp.arange(tok, dtype=jnp.int32)[None, :] == local[:, None]).astype(BF16)

    own, keep, send = pl.pallas_call(
        pick_kernel,
        in_specs=[vmem()] * 2,
        out_specs=[vmem()] * 3,
        out_shape=[shape((slots, width), BF16)] + [shape((slots, packed_width), BF16)] * 2,
        compiler_params=params(12),
        name="pick",
    )(select, hidden)

    mine = pl.pallas_call(
        add_kernel,
        in_specs=[vmem()] * 2,
        out_specs=vmem(),
        out_shape=shape((slots, packed_width), BF16),
        compiler_params=params(4),
        cost_estimate=cost(64 * MIB),
        name="add",
    )(keep, swap(send, "ctx", 1))

    def load(start, dep):
        return pl.pallas_call(
            lambda *refs: load_kernel(start, *refs),
            in_specs=[anywhere(), anywhere()],
            out_specs=vmem(),
            out_shape=shape((voc, half), BF16),
            scratch_shapes=[pltpu.SemaphoreType.DMA(())],
            compiler_params=params(46),
            cost_estimate=cost(voc * half * 4),
            name="load",
        )(head, dep)

    loads = []
    for k, bit in enumerate(inner_bits):
        at = k - len(inner_bits) + 2
        before = mine
        mine = before + swap(before, "ctx", bit)
        if at >= 0:
            loads.append(load(half * at, before))
    targets = pl.pallas_call(
        lambda *refs: targets_kernel(voc, *refs),
        in_specs=[smem(), anywhere()],
        out_specs=vmem(),
        out_shape=shape((total, LANES), jnp.int32),
        compiler_params=params(4),
        name="targets",
    )(masked_targets, mine)
    there = swap(mine, "ctx", blocks)

    def squares_of(x):
        part = jnp.sum(x[:, half : half + 3].astype(F32), axis=1, keepdims=True)
        return jnp.broadcast_to(part, (slots, LANES))

    mine_squares = squares_of(mine)
    mine_other = swap(mine, "ctx", 1)
    ways = lax.axis_size("vocab")
    if ways == 2:
        across = lax.ppermute(
            mine_squares,
            ("ctx", "vocab"),
            [(i, i ^ (blocks * ways + 1)) for i in range(count * ways)],
        )
        mine_squares = mine_squares + swap(mine_squares, "vocab", 1)
        there_squares = squares_of(there) + across
    else:
        mine_squares = sum_over(mine_squares, "vocab")
        there_squares = sum_over(squares_of(there), "vocab")
    there_other = swap(there, "ctx", 1)
    left, right, scaled, inverse = pl.pallas_call(
        lambda *refs: normalize_kernel(blocks, model_width, *refs),
        in_specs=[vmem()] * 7,
        out_specs=[vmem()] * 4,
        out_shape=[
            shape((total, half), BF16),
            shape((total, half), BF16),
            shape((total, width), F32),
            shape((total, LANES), F32),
        ],
        compiler_params=params(8),
        name="normalize",
    )(mine, mine_other, there, there_other, mine_squares, there_squares, gain_row)

    partial = sum(
        lax.dot_general(a, b, (((1,), (1,)), ((), ())), preferred_element_type=F32)
        for a, b in zip((left, right), loads)
    )
    bit = 1
    while 2 * bit < lax.axis_size("vocab"):
        partial = partial + swap(partial, "vocab", bit)
        bit *= 2
    logits, exps, table = pl.pallas_call(
        stats_kernel,
        in_specs=[vmem()] * 3,
        out_specs=[vmem()] * 3,
        out_shape=[
            shape((total, voc), F32),
            shape((2 * total, voc), BF16),
            shape((SUBLANES, LANES), F32),
        ],
        compiler_params=params(8),
        name="stats",
    )(targets, partial, swap(partial, "vocab", bit))

    own_table = table

    def merge(a, b):
        return pl.pallas_call(
            merge_kernel,
            in_specs=[vmem()] * 2,
            out_specs=vmem(),
            out_shape=shape((SUBLANES, LANES), F32),
            compiler_params=params(4),
            name="merge",
        )(a, b)

    bits = [1] + inner_bits
    for bit in bits:
        table = merge(table, swap(table, "ctx", bit))
    there_table = swap(table, "ctx", blocks)
    parts = [jnp.dot(exps, block, preferred_element_type=F32) for block in loads]

    keep, send, meta, loss_value = pl.pallas_call(
        lambda *refs: combine_kernel(tok * blocks, model_width, *refs),
        in_specs=[smem(), smem()] + [vmem()] * 7,
        out_specs=[vmem()] * 4,
        out_shape=[
            shape((total, packed_width), F32),
            shape((total, packed_width), BF16),
            shape((total, LANES), F32),
            shape((1, 1), F32),
        ],
        scratch_shapes=[pltpu.VMEM((total, LANES), F32)]
        + [pltpu.VMEM((SUBLANES, LANES), F32)],
        compiler_params=params(10),
        name="combine",
    )(t_num, t_den, own_table, table, there_table, *parts, scaled, inverse)

    steps = 8
    step = width // steps
    grad_head = None

    def head_part(first, last, dep, so_far):
        extra = [dep] + ([] if so_far is None else [so_far])
        return pl.pallas_call(
            head_kernel,
            grid=(last - first,),
            in_specs=[
                pl.BlockSpec((voc, total), lambda i: (0, 0)),
                pl.BlockSpec((total, step), lambda i: (0, first % (steps // 2) + i)),
            ]
            + [anywhere()] * len(extra),
            out_specs=pl.BlockSpec((voc, step), lambda i: (0, first + i)),
            out_shape=shape((voc, width), BF16),
            input_output_aliases={} if so_far is None else {3: 0},
            compiler_params=params(12),
            cost_estimate=cost(2 * voc * step * (last - first)),
            name="head_grad",
        )(dlogits, right if first >= steps // 2 else left, *extra)

    arrived = swap(send, "ctx", 1)
    own_part, give = pl.pallas_call(
        lambda *refs: divide_kernel(blocks, *refs),
        in_specs=[vmem()] * 2,
        out_specs=[vmem()] * 2,
        out_shape=[shape((slots, packed_width), F32), shape((slots, packed_width), BF16)],
        compiler_params=params(6),
        name="divide",
    )(keep, arrived)
    cuts = [0, 4, 6, 8]
    dlogits = pl.pallas_call(
        dlogits_kernel,
        in_specs=[vmem()] * 3 + [anywhere()],
        out_specs=vmem(),
        out_shape=shape((voc, total), BF16),
        compiler_params=params(6),
        name="dlogits",
    )(targets, logits, meta, give)
    grad_head = head_part(cuts[0], cuts[1], give, None)
    sent = (own_part + swap(give, "ctx", blocks).astype(F32)).astype(BF16)
    for k, bit in enumerate(inner_bits):
        at = k - len(inner_bits) + 2
        before = sent
        sent = before + swap(before, "ctx", bit)
        if at >= 0:
            grad_head = head_part(cuts[at + 1], cuts[at + 2], before, grad_head)
    other = swap(sent, "ctx", 1)

    final_step = half // 2
    grad_hidden, grad_gain = pl.pallas_call(
        lambda *refs: final_kernel(blocks, *refs),
        in_specs=[vmem()] * 7,
        out_specs=[anywhere(), vmem()],
        out_shape=[shape((tok, width), BF16), shape((1, width), F32)],
        scratch_shapes=[
            pltpu.VMEM((width // final_step, tok, final_step), BF16),
            pltpu.SemaphoreType.DMA((width // final_step,)),
        ],
        compiler_params=params(12),
        name="final",
    )(select, sent, other, own, inverse, meta, gain_row)
    return (loss_value.reshape(()), grad_hidden, grad_head, grad_gain.reshape(width))


def solution(mesh):
    placed = (P("ctx", "vocab"), P("vocab"), P("ctx", "vocab"), P(), P(), P(), P())
    return jax.shard_map(
        device_step,
        mesh=mesh,
        in_specs=placed,
        out_specs=(P(), P("ctx", "vocab"), P("ctx", "vocab"), P("vocab")),
        check_vma=False,
    )
```

```python
import jax
import jax.numpy as jnp
from jax import lax
from jax.experimental import pallas as pl
from jax.experimental.pallas import tpu as pltpu
from jax.sharding import PartitionSpec as P


EPSILON = 1e-05
LOSS_SCALE = 1024.0
LANES = 128
SUBLANES = 8
MIB = 1 << 20
F32 = jnp.float32
BF16 = jnp.bfloat16


def vmem():
    return pl.BlockSpec(memory_space=pltpu.VMEM)


def smem():
    return pl.BlockSpec(memory_space=pltpu.SMEM)


def anywhere():
    return pl.BlockSpec(memory_space=pl.ANY)


def params(mib):
    return pltpu.CompilerParams(vmem_limit_bytes=mib * MIB)


def cost(bytes_accessed):
    return pl.CostEstimate(flops=0, bytes_accessed=bytes_accessed, transcendentals=0)


def shape(dims, dtype):
    return jax.ShapeDtypeStruct(dims, dtype)


def swap(x, axis, bit):
    return lax.ppermute(x, axis, [(i, i ^ bit) for i in range(lax.axis_size(axis))])


def sum_over(x, axis):
    bit = 1
    while bit < lax.axis_size(axis):
        x = x + swap(x, axis, bit)
        bit *= 2
    return x


def here(blocks):
    ctx = lax.axis_index("ctx")
    return ctx, ctx // blocks, ctx % blocks, ctx % 2


def three_parts(x):
    high = x.astype(BF16).astype(F32)
    middle = (x - high).astype(BF16).astype(F32)
    low = x - high - middle
    lane = lax.broadcasted_iota(jnp.int32, (x.shape[0], LANES), 1)
    tail = jnp.where(lane == 0, high, jnp.where(lane == 1, middle, jnp.where(lane == 2, low, 0.0)))
    return tail.astype(BF16)


def whole(tail):
    return jnp.sum(tail.astype(F32), axis=1, keepdims=True)


def pick_kernel(rows_ref, own_ref, keep_ref, send_ref, squares_ref):
    half = rows_ref.shape[1] // 2
    core = lax.axis_index("ctx") % 2
    rows = rows_ref[...]
    squares = jnp.sum(rows * rows, axis=1, keepdims=True)
    squares_ref[...] = jnp.broadcast_to(squares, squares_ref.shape)
    tail = three_parts(squares)
    own = rows.astype(BF16)
    own_ref[...] = own
    keep_ref[:, half:] = tail
    send_ref[:, half:] = tail

    @pl.when(core == 0)
    def _():
        keep_ref[:, :half] = own[:, :half]
        send_ref[:, :half] = own[:, half:]

    @pl.when(core == 1)
    def _():
        keep_ref[:, :half] = own[:, half:]
        send_ref[:, :half] = own[:, :half]


def add_kernel(first_ref, second_ref, out_ref, squares_ref):
    half = out_ref.shape[1] - LANES
    out_ref[:, :half] = first_ref[:, :half] + second_ref[:, :half]
    squares = whole(first_ref[:, half:]) + whole(second_ref[:, half:])
    out_ref[:, half:] = three_parts(squares)
    squares_ref[...] = jnp.broadcast_to(squares, squares_ref.shape)


def settle_kernel(first_ref, second_ref, squares_ref, up_ref, across_ref, out_ref):
    half = out_ref.shape[1] - LANES
    out_ref[:, :half] = first_ref[:, :half] + second_ref[:, :half]
    here_squares = squares_ref[:, 0:1] + whole(second_ref[:, half:])
    out_ref[:, half:] = three_parts(here_squares + (up_ref[:, 0:1] + across_ref[:, 0:1]))


def join_kernel(*refs):
    a, b, c, d = (ref[...].astype(F32) for ref in refs[:4])
    refs[4][...] = ((a + b) + (c + d)).astype(refs[4].dtype)


def retail_kernel(first_ref, squares_ref, out_ref):
    half = out_ref.shape[1] - LANES
    out_ref[:, :half] = first_ref[:, :half]
    out_ref[:, half:] = three_parts(squares_ref[:, 0:1])


def load_kernel(side, head_ref, dep_ref, out_ref, sem):
    del dep_ref
    half = out_ref.shape[1]
    start = pl.multiple_of((lax.axis_index("ctx") + side) % 2 * half, LANES)
    copy = pltpu.make_async_copy(head_ref.at[:, pl.ds(start, half)], out_ref, sem)
    copy.start()
    copy.wait()


def normalize_kernel(
    blocks, model_width, side, mine_ref, there_ref, gain_ref, *rest
):
    slots = mine_ref.shape[0]
    half = mine_ref.shape[1] - LANES
    _, seq, _, core = here(blocks)
    normed_ref, scaled_ref = rest[:2]
    gain = gain_ref[:, pl.ds(pl.multiple_of((core + side) % 2 * half, LANES), half)]
    for ref, s in ((mine_ref, seq), (there_ref, 1 - seq)):
        rows = pl.ds(pl.multiple_of(s * slots, slots), slots)
        inverse = lax.rsqrt(whole(ref[:, half:]) / model_width + EPSILON)
        scaled = ref[:, :half].astype(F32) * inverse
        scaled_ref[rows, :] = scaled
        normed_ref[rows, :] = (scaled * gain).astype(BF16)
        if len(rest) == 3:
            rest[2][rows, :] = jnp.broadcast_to(inverse, (slots, LANES))


def targets_kernel(voc, ref, dep_ref, out_ref):
    del dep_ref
    total = out_ref.shape[0]
    slots = total // 2
    place = lax.broadcasted_iota(jnp.int32, out_ref.shape, 0)
    out = jnp.zeros(out_ref.shape, jnp.int32)
    for r in range(total):
        out = jnp.where(place == r, ref[r // slots, r % slots], out)
    out_ref[...] = out - lax.axis_index("ctx") * voc


def stats_kernel(targets_ref, first_ref, second_ref, logits_ref, exps_ref, table_ref):
    total, voc = first_ref.shape
    logits = first_ref[...] + second_ref[...]
    logits_ref[...] = logits
    is_target = lax.broadcasted_iota(jnp.int32, (total, voc), 1) == targets_ref[:, 0:1]
    top = jnp.max(logits, axis=1, keepdims=True)
    away = logits - top
    exps = jnp.exp(away)
    exps_ref[:total, :] = jnp.where(is_target, 0.0, exps).astype(BF16)
    exps_ref[total:, :] = jnp.where(is_target, 1.0, 0.0).astype(BF16)
    entries = (
        top,
        jnp.sum(exps, axis=1, keepdims=True),
        jnp.sum(exps * away, axis=1, keepdims=True),
        jnp.sum(jnp.where(is_target, logits, 0.0), axis=1, keepdims=True),
    )
    lane = lax.broadcasted_iota(jnp.int32, (LANES, LANES), 1)
    table = jnp.zeros((LANES, LANES), F32)
    for k, entry in enumerate(entries):
        entry = jnp.concatenate([entry, jnp.zeros((LANES - total, 1), F32)]) if total < LANES else entry
        table = jnp.where(lane == k, entry, table)
    table_ref[...] = table.T[:SUBLANES, :]


def merged(first, second):
    top = jnp.maximum(first[0:1], second[0:1])
    gap_first = first[0:1] - top
    gap_second = second[0:1] - top
    exp_first = jnp.exp(gap_first)
    exp_second = jnp.exp(gap_second)
    return (
        top,
        first[1:2] * exp_first + second[1:2] * exp_second,
        (first[2:3] + gap_first * first[1:2]) * exp_first
        + (second[2:3] + gap_second * second[1:2]) * exp_second,
        first[3:4] + second[3:4],
    )


def merge_kernel(first_ref, second_ref, out_ref):
    out_ref[...] = jnp.zeros_like(out_ref)
    for k, row in enumerate(merged(first_ref, second_ref)):
        out_ref[k : k + 1, :] = row


def merge_four_kernel(a_ref, b_ref, c_ref, d_ref, out_ref, near_ref, far_ref):
    merge_kernel(a_ref, b_ref, near_ref)
    merge_kernel(c_ref, d_ref, far_ref)
    merge_kernel(near_ref, far_ref, out_ref)


def scaled_part(spread, at_target, part_ref, scaled_ref, out_ref, tail_ref):
    total, half = scaled_ref.shape
    part = spread * part_ref[:total, :] + at_target * part_ref[total:, :]
    gain = jnp.sum(part * scaled_ref[...], axis=0, keepdims=True)
    tail_ref[...] = jnp.zeros_like(tail_ref)
    for j in range(half // LANES):
        tail_ref[j : j + 1, :] = gain[:, j * LANES : (j + 1) * LANES]
    out_ref[:, :half] = part.astype(out_ref.dtype)
    out_ref[:, half:] = tail_ref[...].astype(out_ref.dtype)


def send_kernel(
    length, model_width, num_ref, den_ref, own_ref, a_ref, b_ref, part_ref, scaled_ref,
    inverse_ref, send_ref, meta_ref, loss_ref, tail_ref, rows_ref,
):
    total = inverse_ref.shape[0]
    slots = total // 2
    row_top, exp_total, moment, picked = merged(a_ref, b_ref)
    log_total = row_top + jnp.log(exp_total)
    place = lax.broadcasted_iota(jnp.int32, (1, LANES), 1)
    den = jnp.where(place < slots, den_ref[0], den_ref[1]).astype(F32)
    num = jnp.where(place < slots, num_ref[0], num_ref[1]).astype(F32)
    factor = den / (num * (2.0 * length))
    scale = LOSS_SCALE * factor
    inner = scale * (moment / exp_total - (picked - row_top)) / model_width
    spread = scale * jnp.exp(own_ref[0:1, :] - log_total)
    at_target = scale * (jnp.exp(picked - log_total) - 1.0)
    rows_ref[...] = jnp.zeros_like(rows_ref)
    for k, row in enumerate((log_total, scale, inner, spread, at_target)):
        rows_ref[k : k + 1, :] = row
    across = jnp.concatenate([rows_ref[...], jnp.zeros((LANES - SUBLANES, LANES), F32)]).T[:total]
    scaled_part(across[:, 3:4], across[:, 4:5], part_ref, scaled_ref, send_ref, tail_ref)
    lane = lax.broadcasted_iota(jnp.int32, (total, LANES), 1)
    meta_ref[...] = jnp.where(lane == 2, across / inverse_ref[...], across)
    loss_ref[...] = jnp.sum(
        jnp.where(place < total, factor * (log_total - picked), 0.0), axis=1, keepdims=True
    )


def keep_kernel(meta_ref, part_ref, scaled_ref, keep_ref, tail_ref):
    scaled_part(meta_ref[:, 3:4], meta_ref[:, 4:5], part_ref, scaled_ref, keep_ref, tail_ref)


def divide_kernel(blocks, keep_ref, arrived_ref, own_ref, give_ref):
    slots = own_ref.shape[0]
    half = own_ref.shape[1] - LANES
    _, seq, _, _ = here(blocks)
    tail = (keep_ref[:slots, half:] + arrived_ref[:slots, half:].astype(F32)).astype(BF16)
    for ref, s in ((own_ref, seq), (give_ref, 1 - seq)):
        rows = pl.ds(pl.multiple_of(s * slots, slots), slots)
        part = keep_ref[rows, :half] + arrived_ref[rows, :half].astype(F32)
        ref[:, :half] = part.astype(ref.dtype)
        ref[:, half:] = tail.astype(ref.dtype)


def dlogits_kernel(
    targets_ref, logits_ref, meta_ref, own_ref, other_ref, dep_ref, out_ref, normed_ref
):
    del dep_ref
    total, voc = logits_ref.shape
    is_target = lax.broadcasted_iota(jnp.int32, (total, voc), 1) == targets_ref[:, 0:1]
    softmax = jnp.exp(logits_ref[...] - meta_ref[:, 0:1])
    out_ref[...] = (
        (meta_ref[:, 1:2] * (softmax - jnp.where(is_target, 1.0, 0.0))).T.astype(BF16)
    )
    half = own_ref.shape[1]
    core = lax.axis_index("ctx") % 2
    for side, ref in enumerate((own_ref, other_ref)):
        normed_ref[:, pl.ds(pl.multiple_of((core + side) % 2 * half, LANES), half)] = ref[...]


def head_kernel(dlogits_ref, normed_ref, *rest):
    rest[-1][...] = jnp.dot(
        dlogits_ref[...], normed_ref[...], preferred_element_type=F32
    ).astype(BF16)


def final_kernel(
    blocks, side, select_ref, part_ref, own_ref, inverse_ref, meta_ref, gain_ref, *rest
):
    mine_ref, out_ref, grad_gain_ref, tails_ref = (None, rest[0], None, None)
    if side == 1:
        mine_ref, _, out_ref, grad_gain_ref, tails_ref = rest[:5]
    block_ref, sems = rest[-2:]
    chunks, _, step = block_ref.shape
    slots = part_ref.shape[0]
    half = chunks * step
    _, seq, _, core = here(blocks)
    rows = pl.ds(pl.multiple_of(seq * slots, slots), slots)
    inverse = inverse_ref[rows, :][:, :1]
    pull = inverse * inverse * inverse * meta_ref[rows, :][:, 2:3]
    copies = []
    for chunk in range(chunks):
        start = (core + side) % 2 * half + chunk * step
        columns = pl.ds(pl.multiple_of(start, LANES), step)
        grads = inverse * gain_ref[:, columns] * part_ref[
            :, chunk * step : (chunk + 1) * step
        ].astype(F32) - own_ref[:, columns].astype(F32) * pull
        block_ref[chunk] = lax.dot_general(
            select_ref[...],
            grads.astype(BF16),
            (((0,), (0,)), ((), ())),
            preferred_element_type=F32,
        ).astype(BF16)
        copies.append(
            pltpu.make_async_copy(block_ref.at[chunk], out_ref.at[:, columns], sems.at[chunk])
        )
        copies[-1].start()
    if side == 1:
        a = mine_ref[:, half:].astype(F32)
        b = part_ref[:, half:].astype(F32)
        for start, tail in ((0, jnp.where(core == 0, a, b)), (half, jnp.where(core == 0, b, a))):
            for j in range(half // LANES):
                at = start + j * LANES
                tails_ref[:, at : at + LANES] = tail[j : j + 1, :]
        copies.append(pltpu.make_async_copy(tails_ref, grad_gain_ref, sems.at[chunks]))
        copies[-1].start()
    for copy in copies:
        copy.wait()


def device_step(hidden, norm_gain, head, masked_pos, masked_targets, t_num, t_den):
    tok, width = hidden.shape
    voc = head.shape[0]
    count = lax.axis_size("ctx")
    model_width = width * lax.axis_size("vocab")
    blocks = count // 2
    slots = masked_pos.shape[1]
    total = 2 * slots
    half = width // 2
    packed_width = half + LANES
    inner_bits = [1 << b for b in range(1, count.bit_length() - 2)]
    gain_row = norm_gain.reshape(1, width)

    ctx = lax.axis_index("ctx")
    local = masked_pos[ctx // blocks] - ctx % blocks * tok
    select = (jnp.arange(tok, dtype=jnp.int32)[None, :] == local[:, None]).astype(BF16)

    own, keep, send, squares = pl.pallas_call(
        pick_kernel,
        in_specs=[vmem()],
        out_specs=[vmem()] * 4,
        out_shape=[shape((slots, width), BF16)]
        + [shape((slots, packed_width), BF16)] * 2
        + [shape((slots, LANES), F32)],
        compiler_params=params(6),
        name="pick",
    )(jnp.dot(select, hidden, preferred_element_type=F32))

    ways = lax.axis_size("vocab")

    def load(side, dep):
        return pl.pallas_call(
            lambda *refs: load_kernel(side, *refs),
            in_specs=[anywhere(), anywhere()],
            out_specs=vmem(),
            out_shape=shape((voc, half), BF16),
            scratch_shapes=[pltpu.SemaphoreType.DMA(())],
            compiler_params=params(46),
            cost_estimate=cost(voc * half * 4),
            name="load",
        )(head, dep)

    arrived = swap(send, "ctx", 1)
    loads = [load(0, keep)]
    if ways == 2:
        across = lax.ppermute(
            squares,
            ("ctx", "vocab"),
            [(i, i ^ (ways + 1)) for i in range(count * ways)],
        )
        mine = pl.pallas_call(
            settle_kernel,
            in_specs=[vmem()] * 5,
            out_specs=vmem(),
            out_shape=shape((slots, packed_width), BF16),
            compiler_params=params(4),
            name="settle",
        )(keep, arrived, squares, swap(squares, "vocab", 1), across)
    else:
        mine, squares = pl.pallas_call(
            add_kernel,
            in_specs=[vmem()] * 2,
            out_specs=[vmem()] * 2,
            out_shape=[shape((slots, packed_width), BF16), shape((slots, LANES), F32)],
            compiler_params=params(4),
            name="add",
        )(keep, arrived)
        mine = pl.pallas_call(
            retail_kernel,
            in_specs=[vmem()] * 2,
            out_specs=vmem(),
            out_shape=shape((slots, packed_width), BF16),
            compiler_params=params(4),
            name="retail",
        )(mine, sum_over(squares, "vocab"))

    def around(x):
        first, second = inner_bits[-2:]
        bits = (first, second, first + second)
        return [swap(x, "ctx", bit) for bit in bits]

    def join(x, others):
        return pl.pallas_call(
            join_kernel,
            in_specs=[vmem()] * 4,
            out_specs=vmem(),
            out_shape=shape(x.shape, x.dtype),
            compiler_params=params(4),
            name="join",
        )(x, *others)

    for bit in inner_bits[:-2]:
        mine = mine + swap(mine, "ctx", bit)
    before = mine
    mine = join(before, around(before))
    loads.append(load(1, before))
    there = swap(mine, "ctx", blocks)
    mine_other = swap(mine, "ctx", 1)
    there_other = swap(there, "ctx", 1)

    def normalize(side, a, b):
        extra = [shape((total, LANES), F32)] if side == 0 else []
        return pl.pallas_call(
            lambda *refs: normalize_kernel(blocks, model_width, side, *refs),
            in_specs=[vmem()] * 3,
            out_specs=[vmem()] * (2 + len(extra)),
            out_shape=[shape((total, half), BF16), shape((total, half), F32)] + extra,
            compiler_params=params(6),
            name="normalize",
        )(a, b, gain_row)

    def contract(a, b):
        return lax.dot_general(a, b, (((1,), (1,)), ((), ())), preferred_element_type=F32)

    normed, scaled, inverse = normalize(0, mine, there)
    partial = contract(normed, loads[0])
    normed_other, scaled_other = normalize(1, mine_other, there_other)
    partial = partial + contract(normed_other, loads[1])
    bit = 1
    while 2 * bit < lax.axis_size("vocab"):
        partial = partial + swap(partial, "vocab", bit)
        bit *= 2
    targets = pl.pallas_call(
        lambda *refs: targets_kernel(voc, *refs),
        in_specs=[smem(), anywhere()],
        out_specs=vmem(),
        out_shape=shape((total, LANES), jnp.int32),
        compiler_params=params(4),
        name="targets",
    )(masked_targets, partial)
    logits, exps, table = pl.pallas_call(
        stats_kernel,
        in_specs=[vmem()] * 3,
        out_specs=[vmem()] * 3,
        out_shape=[
            shape((total, voc), F32),
            shape((2 * total, voc), BF16),
            shape((SUBLANES, LANES), F32),
        ],
        compiler_params=params(8),
        name="stats",
    )(targets, partial, swap(partial, "vocab", bit))

    own_table = table

    def merge(a, b):
        return pl.pallas_call(
            merge_kernel,
            in_specs=[vmem()] * 2,
            out_specs=vmem(),
            out_shape=shape((SUBLANES, LANES), F32),
            compiler_params=params(4),
            name="merge",
        )(a, b)

    for bit in [1] + inner_bits[:-2]:
        table = merge(table, swap(table, "ctx", bit))
    near = [table] + around(table)
    table = pl.pallas_call(
        merge_four_kernel,
        in_specs=[vmem()] * 4,
        out_specs=vmem(),
        out_shape=shape((SUBLANES, LANES), F32),
        scratch_shapes=[pltpu.VMEM((SUBLANES, LANES), F32)] * 2,
        compiler_params=params(4),
        name="merge_four",
    )(*near)
    there_table = swap(table, "ctx", blocks)
    part = jnp.dot(exps, loads[0], preferred_element_type=F32)
    part_other = jnp.dot(exps, loads[1], preferred_element_type=F32)
    send, meta, loss_value = pl.pallas_call(
        lambda *refs: send_kernel(tok * blocks, model_width, *refs),
        in_specs=[smem(), smem()] + [vmem()] * 6,
        out_specs=[vmem()] * 3,
        out_shape=[
            shape((total, packed_width), BF16),
            shape((total, LANES), F32),
            shape((1, 1), F32),
        ],
        scratch_shapes=[pltpu.VMEM((total, LANES), F32), pltpu.VMEM((SUBLANES, LANES), F32)],
        compiler_params=params(8),
        name="send_part",
    )(t_num, t_den, own_table, table, there_table, part_other, scaled_other, inverse)
    keep = pl.pallas_call(
        keep_kernel,
        in_specs=[vmem()] * 3,
        out_specs=vmem(),
        out_shape=shape((total, packed_width), F32),
        scratch_shapes=[pltpu.VMEM((total, LANES), F32)],
        compiler_params=params(8),
        name="keep_part",
    )(meta, part, scaled)

    steps = 8
    step = width // steps
    grad_head = None

    def head_part(first, last, dep, so_far):
        extra = [dep] + ([] if so_far is None else [so_far])
        return pl.pallas_call(
            head_kernel,
            grid=(last - first,),
            in_specs=[
                pl.BlockSpec((voc, total), lambda i: (0, 0)),
                pl.BlockSpec((total, step), lambda i: (0, first + i)),
            ]
            + [anywhere()] * len(extra),
            out_specs=pl.BlockSpec((voc, step), lambda i: (0, first + i)),
            out_shape=shape((voc, width), BF16),
            input_output_aliases={} if so_far is None else {3: 0},
            compiler_params=params(12),
            cost_estimate=cost(2 * voc * step * (last - first)),
            name="head_grad",
        )(dlogits, normed, *extra)

    arrived = swap(send, "ctx", 1)
    own_part, give = pl.pallas_call(
        lambda *refs: divide_kernel(blocks, *refs),
        in_specs=[vmem()] * 2,
        out_specs=[vmem()] * 2,
        out_shape=[shape((slots, packed_width), F32), shape((slots, packed_width), BF16)],
        compiler_params=params(6),
        name="divide",
    )(keep, arrived)
    dlogits, normed = pl.pallas_call(
        dlogits_kernel,
        in_specs=[vmem()] * 5 + [anywhere()],
        out_specs=[vmem()] * 2,
        out_shape=[shape((voc, total), BF16), shape((total, width), BF16)],
        compiler_params=params(6),
        name="dlogits",
    )(targets, logits, meta, normed, normed_other, send)
    middle = steps // 2
    grad_head = head_part(0, middle, give, None)
    sent = (own_part + swap(give, "ctx", blocks).astype(F32)).astype(BF16)
    for bit in inner_bits[:-2]:
        sent = sent + swap(sent, "ctx", bit)
    grad_head = head_part(middle, steps, sent, grad_head)
    sent = join(sent, around(sent))
    other = swap(sent, "ctx", 1)

    def finish(side, part, *extra):
        chunks = 4
        return pl.pallas_call(
            lambda *refs: final_kernel(blocks, side, *refs),
            in_specs=[vmem()] * 6 + ([vmem(), anywhere()] if side else []),
            out_specs=[anywhere()] * (1 + side),
            out_shape=[shape((tok, width), BF16)] + ([shape((1, width), F32)] if side else []),
            input_output_aliases={7: 0} if side else {},
            scratch_shapes=[pltpu.VMEM((1, width), F32)] * side
            + [
                pltpu.VMEM((chunks, tok, half // chunks), BF16),
                pltpu.SemaphoreType.DMA((chunks + side,)),
            ],
            compiler_params=params(8),
            name="final",
        )(select, part, own, inverse, meta, gain_row, *extra)

    (grad_hidden,) = finish(0, sent)
    grad_hidden, grad_gain = finish(1, other, sent, grad_hidden)
    return (loss_value.reshape(()), grad_hidden, grad_head, grad_gain.reshape(width))


def solution(mesh):
    placed = (P("ctx", "vocab"), P("vocab"), P("ctx", "vocab"), P(), P(), P(), P())
    return jax.shard_map(
        device_step,
        mesh=mesh,
        in_specs=placed,
        out_specs=(P(), P("ctx", "vocab"), P("ctx", "vocab"), P("vocab")),
        check_vma=False,
    )
```

```python
import jax
import jax.numpy as jnp
from jax import lax
from jax.experimental import pallas as pl
from jax.experimental.pallas import tpu as pltpu
from jax.sharding import PartitionSpec as P


EPSILON = 1e-05
LOSS_SCALE = 1024.0
LANES = 128
SUBLANES = 8
MIB = 1 << 20
F32 = jnp.float32
BF16 = jnp.bfloat16


def vmem():
    return pl.BlockSpec(memory_space=pltpu.VMEM)


def smem():
    return pl.BlockSpec(memory_space=pltpu.SMEM)


def anywhere():
    return pl.BlockSpec(memory_space=pl.ANY)


def params(mib):
    return pltpu.CompilerParams(vmem_limit_bytes=mib * MIB)


def cost(bytes_accessed):
    return pl.CostEstimate(flops=0, bytes_accessed=bytes_accessed, transcendentals=0)


def shape(dims, dtype):
    return jax.ShapeDtypeStruct(dims, dtype)


def swap(x, axis, bit):
    return lax.ppermute(x, axis, [(i, i ^ bit) for i in range(lax.axis_size(axis))])


def sum_over(x, axis):
    bit = 1
    while bit < lax.axis_size(axis):
        x = x + swap(x, axis, bit)
        bit *= 2
    return x


def here(blocks):
    ctx = lax.axis_index("ctx")
    return ctx, ctx // blocks, ctx % blocks, ctx % 2


def three_parts(x):
    high = x.astype(BF16).astype(F32)
    middle = (x - high).astype(BF16).astype(F32)
    low = x - high - middle
    lane = lax.broadcasted_iota(jnp.int32, (x.shape[0], LANES), 1)
    tail = jnp.where(lane == 0, high, jnp.where(lane == 1, middle, jnp.where(lane == 2, low, 0.0)))
    return tail.astype(BF16)


def whole(tail):
    return jnp.sum(tail.astype(F32), axis=1, keepdims=True)


def pick_kernel(rows_ref, own_ref, keep_ref, send_ref, squares_ref):
    half = rows_ref.shape[1] // 2
    core = lax.axis_index("ctx") % 2
    rows = rows_ref[...]
    squares = jnp.sum(rows * rows, axis=1, keepdims=True)
    squares_ref[...] = jnp.broadcast_to(squares, squares_ref.shape)
    tail = three_parts(squares)
    own = rows.astype(BF16)
    own_ref[...] = own
    keep_ref[:, half:] = tail
    send_ref[:, half:] = tail

    @pl.when(core == 0)
    def _():
        keep_ref[:, :half] = own[:, :half]
        send_ref[:, :half] = own[:, half:]

    @pl.when(core == 1)
    def _():
        keep_ref[:, :half] = own[:, half:]
        send_ref[:, :half] = own[:, :half]


def add_kernel(first_ref, second_ref, out_ref, squares_ref):
    half = out_ref.shape[1] - LANES
    out_ref[:, :half] = first_ref[:, :half] + second_ref[:, :half]
    squares = whole(first_ref[:, half:]) + whole(second_ref[:, half:])
    out_ref[:, half:] = three_parts(squares)
    squares_ref[...] = jnp.broadcast_to(squares, squares_ref.shape)


def settle_kernel(first_ref, second_ref, squares_ref, up_ref, across_ref, out_ref):
    half = out_ref.shape[1] - LANES
    out_ref[:, :half] = first_ref[:, :half] + second_ref[:, :half]
    here_squares = squares_ref[:, 0:1] + whole(second_ref[:, half:])
    out_ref[:, half:] = three_parts(here_squares + (up_ref[:, 0:1] + across_ref[:, 0:1]))


def join_kernel(*refs):
    a, b, c, d = (ref[...].astype(F32) for ref in refs[:4])
    refs[4][...] = ((a + b) + (c + d)).astype(refs[4].dtype)


def retail_kernel(first_ref, squares_ref, out_ref):
    half = out_ref.shape[1] - LANES
    out_ref[:, :half] = first_ref[:, :half]
    out_ref[:, half:] = three_parts(squares_ref[:, 0:1])


def load_kernel(side, head_ref, dep_ref, out_ref, sem):
    del dep_ref
    half = out_ref.shape[1]
    start = pl.multiple_of((lax.axis_index("ctx") + side) % 2 * half, LANES)
    copy = pltpu.make_async_copy(head_ref.at[:, pl.ds(start, half)], out_ref, sem)
    copy.start()
    copy.wait()


def normalize_kernel(
    blocks, model_width, side, mine_ref, there_ref, gain_ref, *rest
):
    slots = mine_ref.shape[0]
    half = mine_ref.shape[1] - LANES
    _, seq, _, core = here(blocks)
    normed_ref, scaled_ref = rest[:2]
    gain = gain_ref[:, pl.ds(pl.multiple_of((core + side) % 2 * half, LANES), half)]
    for ref, s in ((mine_ref, seq), (there_ref, 1 - seq)):
        rows = pl.ds(pl.multiple_of(s * slots, slots), slots)
        inverse = lax.rsqrt(whole(ref[:, half:]) / model_width + EPSILON)
        scaled = ref[:, :half].astype(F32) * inverse
        scaled_ref[rows, :] = scaled
        normed_ref[rows, :] = (scaled * gain).astype(BF16)
        if len(rest) == 3:
            rest[2][rows, :] = jnp.broadcast_to(inverse, (slots, LANES))


def targets_kernel(voc, ref, dep_ref, out_ref):
    del dep_ref
    total = out_ref.shape[0]
    slots = total // 2
    place = lax.broadcasted_iota(jnp.int32, out_ref.shape, 0)
    out = jnp.zeros(out_ref.shape, jnp.int32)
    for r in range(total):
        out = jnp.where(place == r, ref[r // slots, r % slots], out)
    out_ref[...] = out - lax.axis_index("ctx") * voc


def stats_kernel(targets_ref, first_ref, second_ref, logits_ref, exps_ref, table_ref):
    total, voc = first_ref.shape
    logits = first_ref[...] + second_ref[...]
    logits_ref[...] = logits
    is_target = lax.broadcasted_iota(jnp.int32, (total, voc), 1) == targets_ref[:, 0:1]
    top = jnp.max(logits, axis=1, keepdims=True)
    away = logits - top
    exps = jnp.exp(away)
    exps_ref[:total, :] = jnp.where(is_target, 0.0, exps).astype(BF16)
    exps_ref[total:, :] = jnp.where(is_target, 1.0, 0.0).astype(BF16)
    entries = (
        top,
        jnp.sum(exps, axis=1, keepdims=True),
        jnp.sum(exps * away, axis=1, keepdims=True),
        jnp.sum(jnp.where(is_target, logits, 0.0), axis=1, keepdims=True),
    )
    lane = lax.broadcasted_iota(jnp.int32, (LANES, LANES), 1)
    table = jnp.zeros((LANES, LANES), F32)
    for k, entry in enumerate(entries):
        entry = jnp.concatenate([entry, jnp.zeros((LANES - total, 1), F32)]) if total < LANES else entry
        table = jnp.where(lane == k, entry, table)
    table_ref[...] = table.T[:SUBLANES, :]


def merged(first, second):
    top = jnp.maximum(first[0:1], second[0:1])
    gap_first = first[0:1] - top
    gap_second = second[0:1] - top
    exp_first = jnp.exp(gap_first)
    exp_second = jnp.exp(gap_second)
    return (
        top,
        first[1:2] * exp_first + second[1:2] * exp_second,
        (first[2:3] + gap_first * first[1:2]) * exp_first
        + (second[2:3] + gap_second * second[1:2]) * exp_second,
        first[3:4] + second[3:4],
    )


def merge_kernel(first_ref, second_ref, out_ref):
    out_ref[...] = jnp.zeros_like(out_ref)
    for k, row in enumerate(merged(first_ref, second_ref)):
        out_ref[k : k + 1, :] = row


def merge_four_kernel(a_ref, b_ref, c_ref, d_ref, out_ref, near_ref, far_ref):
    merge_kernel(a_ref, b_ref, near_ref)
    merge_kernel(c_ref, d_ref, far_ref)
    merge_kernel(near_ref, far_ref, out_ref)


def gradient_kernel(
    blocks, length, model_width, num_ref, den_ref, own_ref, peer_ref, a_ref, b_ref, part_ref,
    peer_part_ref, scaled_ref, inverse_ref, mine_ref, give_ref, meta_ref, loss_ref, rows_ref,
    part_scratch, tail_ref,
):
    total, half = scaled_ref.shape
    slots = total // 2
    _, seq, _, _ = here(blocks)
    row_top, exp_total, moment, picked = merged(a_ref, b_ref)
    log_total = row_top + jnp.log(exp_total)
    place = lax.broadcasted_iota(jnp.int32, (1, LANES), 1)
    den = jnp.where(place < slots, den_ref[0], den_ref[1]).astype(F32)
    num = jnp.where(place < slots, num_ref[0], num_ref[1]).astype(F32)
    factor = den / (num * (2.0 * length))
    scale = LOSS_SCALE * factor
    inner = scale * (moment / exp_total - (picked - row_top)) / model_width
    rows_ref[...] = jnp.zeros_like(rows_ref)
    for k, row in enumerate(
        (
            log_total,
            scale,
            inner,
            scale * jnp.exp(own_ref[0:1, :] - log_total),
            scale * jnp.exp(peer_ref[0:1, :] - log_total),
            scale * (jnp.exp(picked - log_total) - 1.0),
        )
    ):
        rows_ref[k : k + 1, :] = row
    across = jnp.concatenate([rows_ref[...], jnp.zeros((LANES - SUBLANES, LANES), F32)]).T[:total]
    part = (
        across[:, 3:4] * part_ref[:total, :]
        + across[:, 4:5] * peer_part_ref[:total, :].astype(F32)
        + across[:, 5:6] * (part_ref[total:, :] + peer_part_ref[total:, :].astype(F32))
    )
    part_scratch[...] = part
    gain = jnp.sum(part * scaled_ref[...], axis=0, keepdims=True)
    tail_ref[...] = jnp.zeros_like(tail_ref)
    for j in range(half // LANES):
        tail_ref[j : j + 1, :] = gain[:, j * LANES : (j + 1) * LANES]
    tail = tail_ref[...].astype(BF16)
    for ref, s in ((mine_ref, seq), (give_ref, 1 - seq)):
        rows = pl.ds(pl.multiple_of(s * slots, slots), slots)
        ref[:, :half] = part_scratch[rows, :].astype(ref.dtype)
        ref[:, half:] = tail.astype(ref.dtype)
    lane = lax.broadcasted_iota(jnp.int32, (total, LANES), 1)
    meta_ref[...] = jnp.where(lane == 2, across / inverse_ref[...], across)
    loss_ref[...] = jnp.sum(
        jnp.where(place < total, factor * (log_total - picked), 0.0), axis=1, keepdims=True
    )


def dlogits_kernel(
    targets_ref, logits_ref, meta_ref, own_ref, other_ref, dep_ref, out_ref, normed_ref
):
    del dep_ref
    total, voc = logits_ref.shape
    is_target = lax.broadcasted_iota(jnp.int32, (total, voc), 1) == targets_ref[:, 0:1]
    softmax = jnp.exp(logits_ref[...] - meta_ref[:, 0:1])
    out_ref[...] = (
        (meta_ref[:, 1:2] * (softmax - jnp.where(is_target, 1.0, 0.0))).T.astype(BF16)
    )
    half = own_ref.shape[1]
    core = lax.axis_index("ctx") % 2
    for side, ref in enumerate((own_ref, other_ref)):
        normed_ref[:, pl.ds(pl.multiple_of((core + side) % 2 * half, LANES), half)] = ref[...]


def head_kernel(dlogits_ref, normed_ref, *rest):
    rest[-1][...] = jnp.dot(
        dlogits_ref[...], normed_ref[...], preferred_element_type=F32
    ).astype(BF16)


def final_kernel(
    blocks, side, select_ref, part_ref, own_ref, inverse_ref, meta_ref, gain_ref, *rest
):
    mine_ref, out_ref, grad_gain_ref, tails_ref = (None, rest[0], None, None)
    if side == 1:
        mine_ref, _, out_ref, grad_gain_ref, tails_ref = rest[:5]
    block_ref, sems = rest[-2:]
    chunks, _, step = block_ref.shape
    slots = part_ref.shape[0]
    half = chunks * step
    _, seq, _, core = here(blocks)
    rows = pl.ds(pl.multiple_of(seq * slots, slots), slots)
    inverse = inverse_ref[rows, :][:, :1]
    pull = inverse * inverse * inverse * meta_ref[rows, :][:, 2:3]
    copies = []
    for chunk in range(chunks):
        start = (core + side) % 2 * half + chunk * step
        columns = pl.ds(pl.multiple_of(start, LANES), step)
        grads = inverse * gain_ref[:, columns] * part_ref[
            :, chunk * step : (chunk + 1) * step
        ].astype(F32) - own_ref[:, columns].astype(F32) * pull
        block_ref[chunk] = lax.dot_general(
            select_ref[...],
            grads.astype(BF16),
            (((0,), (0,)), ((), ())),
            preferred_element_type=F32,
        ).astype(BF16)
        copies.append(
            pltpu.make_async_copy(block_ref.at[chunk], out_ref.at[:, columns], sems.at[chunk])
        )
        copies[-1].start()
    if side == 1:
        a = mine_ref[:, half:].astype(F32)
        b = part_ref[:, half:].astype(F32)
        for start, tail in ((0, jnp.where(core == 0, a, b)), (half, jnp.where(core == 0, b, a))):
            for j in range(half // LANES):
                at = start + j * LANES
                tails_ref[:, at : at + LANES] = tail[j : j + 1, :]
        copies.append(pltpu.make_async_copy(tails_ref, grad_gain_ref, sems.at[chunks]))
        copies[-1].start()
    for copy in copies:
        copy.wait()


def device_step(hidden, norm_gain, head, masked_pos, masked_targets, t_num, t_den):
    tok, width = hidden.shape
    voc = head.shape[0]
    count = lax.axis_size("ctx")
    model_width = width * lax.axis_size("vocab")
    blocks = count // 2
    slots = masked_pos.shape[1]
    total = 2 * slots
    half = width // 2
    packed_width = half + LANES
    inner_bits = [1 << b for b in range(1, count.bit_length() - 2)]
    gain_row = norm_gain.reshape(1, width)

    ctx = lax.axis_index("ctx")
    local = masked_pos[ctx // blocks] - ctx % blocks * tok
    select = (jnp.arange(tok, dtype=jnp.int32)[None, :] == local[:, None]).astype(BF16)

    own, keep, send, squares = pl.pallas_call(
        pick_kernel,
        in_specs=[vmem()],
        out_specs=[vmem()] * 4,
        out_shape=[shape((slots, width), BF16)]
        + [shape((slots, packed_width), BF16)] * 2
        + [shape((slots, LANES), F32)],
        compiler_params=params(6),
        name="pick",
    )(jnp.dot(select, hidden, preferred_element_type=F32))

    ways = lax.axis_size("vocab")

    def load(side, dep):
        return pl.pallas_call(
            lambda *refs: load_kernel(side, *refs),
            in_specs=[anywhere(), anywhere()],
            out_specs=vmem(),
            out_shape=shape((voc, half), BF16),
            scratch_shapes=[pltpu.SemaphoreType.DMA(())],
            compiler_params=params(46),
            cost_estimate=cost(voc * half * 4),
            name="load",
        )(head, dep)

    arrived = swap(send, "ctx", 1)
    loads = [load(0, keep)]
    if ways == 2:
        across = lax.ppermute(
            squares,
            ("ctx", "vocab"),
            [(i, i ^ (ways + 1)) for i in range(count * ways)],
        )
        mine = pl.pallas_call(
            settle_kernel,
            in_specs=[vmem()] * 5,
            out_specs=vmem(),
            out_shape=shape((slots, packed_width), BF16),
            compiler_params=params(4),
            name="settle",
        )(keep, arrived, squares, swap(squares, "vocab", 1), across)
    else:
        mine, squares = pl.pallas_call(
            add_kernel,
            in_specs=[vmem()] * 2,
            out_specs=[vmem()] * 2,
            out_shape=[shape((slots, packed_width), BF16), shape((slots, LANES), F32)],
            compiler_params=params(4),
            name="add",
        )(keep, arrived)
        mine = pl.pallas_call(
            retail_kernel,
            in_specs=[vmem()] * 2,
            out_specs=vmem(),
            out_shape=shape((slots, packed_width), BF16),
            compiler_params=params(4),
            name="retail",
        )(mine, sum_over(squares, "vocab"))

    def around(x):
        first, second = inner_bits[-2:]
        bits = (first, second, first + second)
        return [swap(x, "ctx", bit) for bit in bits]

    def join(x, others):
        return pl.pallas_call(
            join_kernel,
            in_specs=[vmem()] * 4,
            out_specs=vmem(),
            out_shape=shape(x.shape, x.dtype),
            compiler_params=params(4),
            name="join",
        )(x, *others)

    for bit in inner_bits[:-2]:
        mine = mine + swap(mine, "ctx", bit)
    before = mine
    mine = join(before, around(before))
    loads.append(load(1, before))
    there = swap(mine, "ctx", blocks)
    mine_other = swap(mine, "ctx", 1)
    there_other = swap(there, "ctx", 1)

    def normalize(side, a, b):
        extra = [shape((total, LANES), F32)] if side == 0 else []
        return pl.pallas_call(
            lambda *refs: normalize_kernel(blocks, model_width, side, *refs),
            in_specs=[vmem()] * 3,
            out_specs=[vmem()] * (2 + len(extra)),
            out_shape=[shape((total, half), BF16), shape((total, half), F32)] + extra,
            compiler_params=params(6),
            name="normalize",
        )(a, b, gain_row)

    def contract(a, b):
        return lax.dot_general(a, b, (((1,), (1,)), ((), ())), preferred_element_type=F32)

    normed, scaled, inverse = normalize(0, mine, there)
    partial = contract(normed, loads[0])
    normed_other, _ = normalize(1, mine_other, there_other)
    partial = partial + contract(normed_other, loads[1])
    bit = 1
    while 2 * bit < lax.axis_size("vocab"):
        partial = partial + swap(partial, "vocab", bit)
        bit *= 2
    targets = pl.pallas_call(
        lambda *refs: targets_kernel(voc, *refs),
        in_specs=[smem(), anywhere()],
        out_specs=vmem(),
        out_shape=shape((total, LANES), jnp.int32),
        compiler_params=params(4),
        name="targets",
    )(masked_targets, partial)
    logits, exps, table = pl.pallas_call(
        stats_kernel,
        in_specs=[vmem()] * 3,
        out_specs=[vmem()] * 3,
        out_shape=[
            shape((total, voc), F32),
            shape((2 * total, voc), BF16),
            shape((SUBLANES, LANES), F32),
        ],
        compiler_params=params(8),
        name="stats",
    )(targets, partial, swap(partial, "vocab", bit))

    own_table = table

    def merge(a, b):
        return pl.pallas_call(
            merge_kernel,
            in_specs=[vmem()] * 2,
            out_specs=vmem(),
            out_shape=shape((SUBLANES, LANES), F32),
            compiler_params=params(4),
            name="merge",
        )(a, b)

    peer_table = swap(table, "ctx", 1)
    table = merge(table, peer_table)
    for bit in inner_bits[:-2]:
        table = merge(table, swap(table, "ctx", bit))
    near = [table] + around(table)
    table = pl.pallas_call(
        merge_four_kernel,
        in_specs=[vmem()] * 4,
        out_specs=vmem(),
        out_shape=shape((SUBLANES, LANES), F32),
        scratch_shapes=[pltpu.VMEM((SUBLANES, LANES), F32)] * 2,
        compiler_params=params(4),
        name="merge_four",
    )(*near)
    there_table = swap(table, "ctx", blocks)
    part_other = jnp.dot(exps, loads[1], preferred_element_type=F32).astype(BF16)
    part = jnp.dot(exps, loads[0], preferred_element_type=F32)
    peer_part = swap(part_other, "ctx", 1)
    own_part, give, meta, loss_value = pl.pallas_call(
        lambda *refs: gradient_kernel(blocks, tok * blocks, model_width, *refs),
        in_specs=[smem(), smem()] + [vmem()] * 8,
        out_specs=[vmem()] * 4,
        out_shape=[
            shape((slots, packed_width), F32),
            shape((slots, packed_width), BF16),
            shape((total, LANES), F32),
            shape((1, 1), F32),
        ],
        scratch_shapes=[
            pltpu.VMEM((SUBLANES, LANES), F32),
            pltpu.VMEM((total, half), F32),
            pltpu.VMEM((slots, LANES), F32),
        ],
        compiler_params=params(8),
        name="gradient",
    )(t_num, t_den, own_table, peer_table, table, there_table, part, peer_part, scaled, inverse)

    steps = 4
    step = width // steps
    grad_head = None

    def head_part(first, last, dep, so_far):
        extra = [dep] + ([] if so_far is None else [so_far])
        return pl.pallas_call(
            head_kernel,
            grid=(last - first,),
            in_specs=[
                pl.BlockSpec((voc, total), lambda i: (0, 0)),
                pl.BlockSpec((total, step), lambda i: (0, first + i)),
            ]
            + [anywhere()] * len(extra),
            out_specs=pl.BlockSpec((voc, step), lambda i: (0, first + i)),
            out_shape=shape((voc, width), BF16),
            input_output_aliases={} if so_far is None else {3: 0},
            compiler_params=params(12),
            cost_estimate=cost(2 * voc * step * (last - first)),
            name="head_grad",
        )(dlogits, normed, *extra)

    dlogits, normed = pl.pallas_call(
        dlogits_kernel,
        in_specs=[vmem()] * 5 + [anywhere()],
        out_specs=[vmem()] * 2,
        out_shape=[shape((voc, total), BF16), shape((total, width), BF16)],
        compiler_params=params(6),
        name="dlogits",
    )(targets, logits, meta, normed, normed_other, give)
    middle = 2
    grad_head = head_part(0, middle, give, None)
    sent = (own_part + swap(give, "ctx", blocks).astype(F32)).astype(BF16)
    for bit in inner_bits[:-2]:
        sent = sent + swap(sent, "ctx", bit)
    grad_head = head_part(middle, steps, sent, grad_head)
    sent = join(sent, around(sent))
    other = swap(sent, "ctx", 1)

    def finish(side, part, *extra):
        chunks = 4
        return pl.pallas_call(
            lambda *refs: final_kernel(blocks, side, *refs),
            in_specs=[vmem()] * 6 + ([vmem(), anywhere()] if side else []),
            out_specs=[anywhere()] * (1 + side),
            out_shape=[shape((tok, width), BF16)] + ([shape((1, width), F32)] if side else []),
            input_output_aliases={7: 0} if side else {},
            scratch_shapes=[pltpu.VMEM((1, width), F32)] * side
            + [
                pltpu.VMEM((chunks, tok, half // chunks), BF16),
                pltpu.SemaphoreType.DMA((chunks + side,)),
            ],
            compiler_params=params(8),
            name="final",
        )(select, part, own, inverse, meta, gain_row, *extra)

    (grad_hidden,) = finish(0, sent)
    grad_hidden, grad_gain = finish(1, other, sent, grad_hidden)
    return (loss_value.reshape(()), grad_hidden, grad_head, grad_gain.reshape(width))


def solution(mesh):
    placed = (P("ctx", "vocab"), P("vocab"), P("ctx", "vocab"), P(), P(), P(), P())
    return jax.shard_map(
        device_step,
        mesh=mesh,
        in_specs=placed,
        out_specs=(P(), P("ctx", "vocab"), P("ctx", "vocab"), P("vocab")),
        check_vma=False,
    )
```

```python
import jax
import jax.numpy as jnp
from jax import lax
from jax.experimental import pallas as pl
from jax.experimental.pallas import tpu as pltpu
from jax.sharding import PartitionSpec as P


EPSILON = 1e-05
LOSS_SCALE = 1024.0
LANES = 128
SUBLANES = 8
MIB = 1 << 20
F32 = jnp.float32
BF16 = jnp.bfloat16


def vmem():
    return pl.BlockSpec(memory_space=pltpu.VMEM)


def smem():
    return pl.BlockSpec(memory_space=pltpu.SMEM)


def anywhere():
    return pl.BlockSpec(memory_space=pl.ANY)


def params(mib):
    return pltpu.CompilerParams(vmem_limit_bytes=mib * MIB)


def cost(bytes_accessed):
    return pl.CostEstimate(flops=0, bytes_accessed=bytes_accessed, transcendentals=0)


def shape(dims, dtype):
    return jax.ShapeDtypeStruct(dims, dtype)


def swap(x, axis, bit):
    return lax.ppermute(x, axis, [(i, i ^ bit) for i in range(lax.axis_size(axis))])


def sum_over(x, axis):
    bit = 1
    while bit < lax.axis_size(axis):
        x = x + swap(x, axis, bit)
        bit *= 2
    return x


def here(blocks):
    ctx = lax.axis_index("ctx")
    return ctx, ctx // blocks, ctx % blocks, ctx % 2


def three_parts(x):
    high = x.astype(BF16).astype(F32)
    middle = (x - high).astype(BF16).astype(F32)
    low = x - high - middle
    lane = lax.broadcasted_iota(jnp.int32, (x.shape[0], LANES), 1)
    tail = jnp.where(lane == 0, high, jnp.where(lane == 1, middle, jnp.where(lane == 2, low, 0.0)))
    return tail.astype(BF16)


def whole(tail):
    return jnp.sum(tail.astype(F32), axis=1, keepdims=True)


def pick_kernel(rows_ref, own_ref, keep_ref, send_ref, squares_ref):
    half = rows_ref.shape[1] // 2
    core = lax.axis_index("ctx") % 2
    rows = rows_ref[...]
    squares = jnp.sum(rows * rows, axis=1, keepdims=True)
    squares_ref[...] = jnp.broadcast_to(squares, squares_ref.shape)
    tail = three_parts(squares)
    own = rows.astype(BF16)
    own_ref[...] = own
    keep_ref[:, half:] = tail
    send_ref[:, half:] = tail

    @pl.when(core == 0)
    def _():
        keep_ref[:, :half] = own[:, :half]
        send_ref[:, :half] = own[:, half:]

    @pl.when(core == 1)
    def _():
        keep_ref[:, :half] = own[:, half:]
        send_ref[:, :half] = own[:, :half]


def add_kernel(first_ref, second_ref, out_ref, squares_ref):
    half = out_ref.shape[1] - LANES
    out_ref[:, :half] = first_ref[:, :half] + second_ref[:, :half]
    squares = whole(first_ref[:, half:]) + whole(second_ref[:, half:])
    out_ref[:, half:] = three_parts(squares)
    squares_ref[...] = jnp.broadcast_to(squares, squares_ref.shape)


def settle_kernel(first_ref, second_ref, squares_ref, up_ref, across_ref, out_ref):
    half = out_ref.shape[1] - LANES
    out_ref[:, :half] = first_ref[:, :half] + second_ref[:, :half]
    here_squares = squares_ref[:, 0:1] + whole(second_ref[:, half:])
    out_ref[:, half:] = three_parts(here_squares + (up_ref[:, 0:1] + across_ref[:, 0:1]))


def join_kernel(*refs):
    a, b, c, d = (ref[...].astype(F32) for ref in refs[:4])
    refs[4][...] = ((a + b) + (c + d)).astype(refs[4].dtype)


def retail_kernel(first_ref, squares_ref, out_ref):
    half = out_ref.shape[1] - LANES
    out_ref[:, :half] = first_ref[:, :half]
    out_ref[:, half:] = three_parts(squares_ref[:, 0:1])


def load_kernel(side, head_ref, dep_ref, out_ref, sem):
    del dep_ref
    half = out_ref.shape[1]
    start = pl.multiple_of((lax.axis_index("ctx") + side) % 2 * half, LANES)
    copy = pltpu.make_async_copy(head_ref.at[:, pl.ds(start, half)], out_ref, sem)
    copy.start()
    copy.wait()


def normalize_kernel(
    blocks, model_width, side, mine_ref, there_ref, gain_ref, *rest
):
    slots = mine_ref.shape[0]
    half = mine_ref.shape[1] - LANES
    _, seq, _, core = here(blocks)
    normed_ref = rest[0]
    gain = gain_ref[:, pl.ds(pl.multiple_of((core + side) % 2 * half, LANES), half)]
    for ref, s in ((mine_ref, seq), (there_ref, 1 - seq)):
        rows = pl.ds(pl.multiple_of(s * slots, slots), slots)
        inverse = lax.rsqrt(whole(ref[:, half:]) / model_width + EPSILON)
        scaled = ref[:, :half].astype(F32) * inverse
        normed_ref[rows, :] = (scaled * gain).astype(BF16)
        if side == 0:
            rest[1][rows, :] = scaled
            rest[2][rows, :] = jnp.broadcast_to(inverse, (slots, LANES))


def targets_kernel(voc, ref, dep_ref, out_ref):
    del dep_ref
    total = out_ref.shape[0]
    slots = total // 2
    place = lax.broadcasted_iota(jnp.int32, out_ref.shape, 0)
    out = jnp.zeros(out_ref.shape, jnp.int32)
    for r in range(total):
        out = jnp.where(place == r, ref[r // slots, r % slots], out)
    out_ref[...] = out - lax.axis_index("ctx") * voc


def stats_kernel(targets_ref, first_ref, second_ref, logits_ref, exps_ref, table_ref):
    total, voc = first_ref.shape
    logits = first_ref[...] + second_ref[...]
    logits_ref[...] = logits
    is_target = lax.broadcasted_iota(jnp.int32, (total, voc), 1) == targets_ref[:, 0:1]
    top = jnp.max(logits, axis=1, keepdims=True)
    away = logits - top
    exps = jnp.exp(away)
    exps_ref[:total, :] = jnp.where(is_target, 0.0, exps).astype(BF16)
    exps_ref[total:, :] = jnp.where(is_target, 1.0, 0.0).astype(BF16)
    entries = (
        top,
        jnp.sum(exps, axis=1, keepdims=True),
        jnp.sum(exps * away, axis=1, keepdims=True),
        jnp.sum(jnp.where(is_target, logits, 0.0), axis=1, keepdims=True),
    )
    lane = lax.broadcasted_iota(jnp.int32, (LANES, LANES), 1)
    table = jnp.zeros((LANES, LANES), F32)
    for k, entry in enumerate(entries):
        entry = jnp.concatenate([entry, jnp.zeros((LANES - total, 1), F32)]) if total < LANES else entry
        table = jnp.where(lane == k, entry, table)
    table_ref[...] = table.T[:SUBLANES, :]


def merged(first, second):
    top = jnp.maximum(first[0:1], second[0:1])
    gap_first = first[0:1] - top
    gap_second = second[0:1] - top
    exp_first = jnp.exp(gap_first)
    exp_second = jnp.exp(gap_second)
    return (
        top,
        first[1:2] * exp_first + second[1:2] * exp_second,
        (first[2:3] + gap_first * first[1:2]) * exp_first
        + (second[2:3] + gap_second * second[1:2]) * exp_second,
        first[3:4] + second[3:4],
    )


def merge_kernel(first_ref, second_ref, out_ref):
    out_ref[...] = jnp.zeros_like(out_ref)
    for k, row in enumerate(merged(first_ref, second_ref)):
        out_ref[k : k + 1, :] = row


def merge_four_kernel(a_ref, b_ref, c_ref, d_ref, out_ref, near_ref, far_ref):
    merge_kernel(a_ref, b_ref, near_ref)
    merge_kernel(c_ref, d_ref, far_ref)
    merge_kernel(near_ref, far_ref, out_ref)


def gradient_kernel(
    blocks, length, model_width, num_ref, den_ref, own_ref, peer_ref, a_ref, b_ref, part_ref,
    peer_part_ref, scaled_ref, inverse_ref, mine_ref, give_ref, meta_ref, rows_ref,
    part_scratch, tail_ref,
):
    total, half = scaled_ref.shape
    slots = total // 2
    _, seq, _, _ = here(blocks)
    row_top, exp_total, moment, picked = merged(a_ref, b_ref)
    log_total = row_top + jnp.log(exp_total)
    place = lax.broadcasted_iota(jnp.int32, (1, LANES), 1)
    den = jnp.where(place < slots, den_ref[0], den_ref[1]).astype(F32)
    num = jnp.where(place < slots, num_ref[0], num_ref[1]).astype(F32)
    factor = den / (num * (2.0 * length))
    scale = LOSS_SCALE * factor
    inner = scale * (moment / exp_total - (picked - row_top)) / model_width
    rows_ref[...] = jnp.zeros_like(rows_ref)
    for k, row in enumerate(
        (
            log_total,
            scale,
            inner,
            scale * jnp.exp(own_ref[0:1, :] - log_total),
            scale * jnp.exp(peer_ref[0:1, :] - log_total),
            scale * (jnp.exp(picked - log_total) - 1.0),
        )
    ):
        rows_ref[k : k + 1, :] = row
    across = jnp.concatenate([rows_ref[...], jnp.zeros((LANES - SUBLANES, LANES), F32)]).T[:total]
    part = (
        across[:, 3:4] * part_ref[:total, :]
        + across[:, 4:5] * peer_part_ref[:total, :].astype(F32)
        + across[:, 5:6] * (part_ref[total:, :] + peer_part_ref[total:, :].astype(F32))
    )
    part_scratch[...] = part
    gain = jnp.sum(part * scaled_ref[...], axis=0, keepdims=True)
    tail_ref[...] = jnp.zeros_like(tail_ref)
    for j in range(half // LANES):
        tail_ref[j : j + 1, :] = gain[:, j * LANES : (j + 1) * LANES]
    tail = tail_ref[...].astype(BF16)
    for ref, s in ((mine_ref, seq), (give_ref, 1 - seq)):
        rows = pl.ds(pl.multiple_of(s * slots, slots), slots)
        ref[:, :half] = part_scratch[rows, :].astype(ref.dtype)
        ref[:, half:] = tail.astype(ref.dtype)
    lane = lax.broadcasted_iota(jnp.int32, (total, LANES), 1)
    loss = jnp.sum(
        jnp.where(place < total, factor * (log_total - picked), 0.0), axis=1, keepdims=True
    )
    meta = jnp.where(lane == 2, across / inverse_ref[...], across)
    meta_ref[...] = jnp.where(lane == 6, loss, meta)


def dlogits_kernel(
    targets_ref, logits_ref, meta_ref, own_ref, other_ref, dep_ref, out_ref, normed_ref
):
    del dep_ref
    total, voc = logits_ref.shape
    is_target = lax.broadcasted_iota(jnp.int32, (total, voc), 1) == targets_ref[:, 0:1]
    softmax = jnp.exp(logits_ref[...] - meta_ref[:, 0:1])
    out_ref[...] = (
        (meta_ref[:, 1:2] * (softmax - jnp.where(is_target, 1.0, 0.0))).T.astype(BF16)
    )
    half = own_ref.shape[1]
    core = lax.axis_index("ctx") % 2
    for side, ref in enumerate((own_ref, other_ref)):
        normed_ref[:, pl.ds(pl.multiple_of((core + side) % 2 * half, LANES), half)] = ref[...]


def loss_kernel(meta_ref, dep_ref, loss_ref):
    del dep_ref
    loss_ref[...] = meta_ref[0:1, 6:7]


def head_kernel(dlogits_ref, normed_ref, *rest):
    rest[-1][...] = jnp.dot(
        dlogits_ref[...], normed_ref[...], preferred_element_type=F32
    ).astype(BF16)


def final_kernel(
    blocks, side, select_ref, part_ref, own_ref, inverse_ref, meta_ref, gain_ref, *rest
):
    mine_ref, out_ref, grad_gain_ref, tails_ref = (None, rest[0], None, None)
    if side == 1:
        mine_ref, _, out_ref, grad_gain_ref, tails_ref = rest[:5]
    block_ref, sems = rest[-2:]
    chunks, _, step = block_ref.shape
    slots = part_ref.shape[0]
    half = chunks * step
    _, seq, _, core = here(blocks)
    rows = pl.ds(pl.multiple_of(seq * slots, slots), slots)
    inverse = inverse_ref[rows, :][:, :1]
    pull = inverse * inverse * inverse * meta_ref[rows, :][:, 2:3]
    copies = []
    for chunk in range(chunks):
        start = (core + side) % 2 * half + chunk * step
        columns = pl.ds(pl.multiple_of(start, LANES), step)
        grads = inverse * gain_ref[:, columns] * part_ref[
            :, chunk * step : (chunk + 1) * step
        ].astype(F32) - own_ref[:, columns].astype(F32) * pull
        block_ref[chunk] = lax.dot_general(
            select_ref[...],
            grads.astype(BF16),
            (((0,), (0,)), ((), ())),
            preferred_element_type=F32,
        ).astype(BF16)
        copies.append(
            pltpu.make_async_copy(block_ref.at[chunk], out_ref.at[:, columns], sems.at[chunk])
        )
        copies[-1].start()
    if side == 1:
        a = mine_ref[:, half:].astype(F32)
        b = part_ref[:, half:].astype(F32)
        for start, tail in ((0, jnp.where(core == 0, a, b)), (half, jnp.where(core == 0, b, a))):
            for j in range(half // LANES):
                at = start + j * LANES
                tails_ref[:, at : at + LANES] = tail[j : j + 1, :]
        copies.append(pltpu.make_async_copy(tails_ref, grad_gain_ref, sems.at[chunks]))
        copies[-1].start()
    for copy in copies:
        copy.wait()


def device_step(hidden, norm_gain, head, masked_pos, masked_targets, t_num, t_den):
    tok, width = hidden.shape
    voc = head.shape[0]
    count = lax.axis_size("ctx")
    model_width = width * lax.axis_size("vocab")
    blocks = count // 2
    slots = masked_pos.shape[1]
    total = 2 * slots
    half = width // 2
    packed_width = half + LANES
    inner_bits = [1 << b for b in range(1, count.bit_length() - 2)]
    gain_row = norm_gain.reshape(1, width)

    ctx = lax.axis_index("ctx")
    local = masked_pos[ctx // blocks] - ctx % blocks * tok
    select = (jnp.arange(tok, dtype=jnp.int32)[None, :] == local[:, None]).astype(BF16)

    own, keep, send, squares = pl.pallas_call(
        pick_kernel,
        in_specs=[vmem()],
        out_specs=[vmem()] * 4,
        out_shape=[shape((slots, width), BF16)]
        + [shape((slots, packed_width), BF16)] * 2
        + [shape((slots, LANES), F32)],
        compiler_params=params(6),
        name="pick",
    )(jnp.dot(select, hidden, preferred_element_type=F32))

    ways = lax.axis_size("vocab")

    def load(side, dep):
        return pl.pallas_call(
            lambda *refs: load_kernel(side, *refs),
            in_specs=[anywhere(), anywhere()],
            out_specs=vmem(),
            out_shape=shape((voc, half), BF16),
            scratch_shapes=[pltpu.SemaphoreType.DMA(())],
            compiler_params=params(46),
            cost_estimate=cost(voc * half * 4),
            name="load",
        )(head, dep)

    arrived = swap(send, "ctx", 1)
    loads = [load(0, keep)]
    if ways == 2:
        across = lax.ppermute(
            squares,
            ("ctx", "vocab"),
            [(i, i ^ (ways + 1)) for i in range(count * ways)],
        )
        mine = pl.pallas_call(
            settle_kernel,
            in_specs=[vmem()] * 5,
            out_specs=vmem(),
            out_shape=shape((slots, packed_width), BF16),
            compiler_params=params(4),
            name="settle",
        )(keep, arrived, squares, swap(squares, "vocab", 1), across)
    else:
        mine, squares = pl.pallas_call(
            add_kernel,
            in_specs=[vmem()] * 2,
            out_specs=[vmem()] * 2,
            out_shape=[shape((slots, packed_width), BF16), shape((slots, LANES), F32)],
            compiler_params=params(4),
            name="add",
        )(keep, arrived)
        mine = pl.pallas_call(
            retail_kernel,
            in_specs=[vmem()] * 2,
            out_specs=vmem(),
            out_shape=shape((slots, packed_width), BF16),
            compiler_params=params(4),
            name="retail",
        )(mine, sum_over(squares, "vocab"))

    def around(x):
        first, second = inner_bits[-2:]
        bits = (first, second, first + second)
        return [swap(x, "ctx", bit) for bit in bits]

    def join(x, others):
        return pl.pallas_call(
            join_kernel,
            in_specs=[vmem()] * 4,
            out_specs=vmem(),
            out_shape=shape(x.shape, x.dtype),
            compiler_params=params(4),
            name="join",
        )(x, *others)

    for bit in inner_bits[:-2]:
        mine = mine + swap(mine, "ctx", bit)
    before = mine
    mine = join(before, around(before))
    loads.append(load(1, mine))
    there = swap(mine, "ctx", blocks)
    mine_other = swap(mine, "ctx", 1)
    there_other = swap(there, "ctx", 1)

    def normalize(side, a, b):
        extra = [] if side else [shape((total, half), F32), shape((total, LANES), F32)]
        return pl.pallas_call(
            lambda *refs: normalize_kernel(blocks, model_width, side, *refs),
            in_specs=[vmem()] * 3,
            out_specs=[vmem()] * (1 + len(extra)),
            out_shape=[shape((total, half), BF16)] + extra,
            compiler_params=params(6),
            name="normalize",
        )(a, b, gain_row)

    def contract(a, b):
        return lax.dot_general(a, b, (((1,), (1,)), ((), ())), preferred_element_type=F32)

    normed, scaled, inverse = normalize(0, mine, there)
    partial = contract(normed, loads[0])
    (normed_other,) = normalize(1, mine_other, there_other)
    partial = partial + contract(normed_other, loads[1])
    bit = 1
    while 2 * bit < lax.axis_size("vocab"):
        partial = partial + swap(partial, "vocab", bit)
        bit *= 2
    targets = pl.pallas_call(
        lambda *refs: targets_kernel(voc, *refs),
        in_specs=[smem(), anywhere()],
        out_specs=vmem(),
        out_shape=shape((total, LANES), jnp.int32),
        compiler_params=params(4),
        name="targets",
    )(masked_targets, partial)
    logits, exps, table = pl.pallas_call(
        stats_kernel,
        in_specs=[vmem()] * 3,
        out_specs=[vmem()] * 3,
        out_shape=[
            shape((total, voc), F32),
            shape((2 * total, voc), BF16),
            shape((SUBLANES, LANES), F32),
        ],
        compiler_params=params(8),
        name="stats",
    )(targets, partial, swap(partial, "vocab", bit))

    own_table = table

    def merge(a, b):
        return pl.pallas_call(
            merge_kernel,
            in_specs=[vmem()] * 2,
            out_specs=vmem(),
            out_shape=shape((SUBLANES, LANES), F32),
            compiler_params=params(4),
            name="merge",
        )(a, b)

    peer_table = swap(table, "ctx", 1)
    table = merge(table, peer_table)
    for bit in inner_bits[:-2]:
        table = merge(table, swap(table, "ctx", bit))
    near = [table] + around(table)
    table = pl.pallas_call(
        merge_four_kernel,
        in_specs=[vmem()] * 4,
        out_specs=vmem(),
        out_shape=shape((SUBLANES, LANES), F32),
        scratch_shapes=[pltpu.VMEM((SUBLANES, LANES), F32)] * 2,
        compiler_params=params(4),
        name="merge_four",
    )(*near)
    there_table = swap(table, "ctx", blocks)
    part_other = jnp.dot(exps, loads[1], preferred_element_type=F32).astype(BF16)
    part = jnp.dot(exps, loads[0], preferred_element_type=F32)
    peer_part = swap(part_other, "ctx", 1)
    own_part, give, meta = pl.pallas_call(
        lambda *refs: gradient_kernel(blocks, tok * blocks, model_width, *refs),
        in_specs=[smem(), smem()] + [vmem()] * 8,
        out_specs=[vmem()] * 3,
        out_shape=[
            shape((slots, packed_width), F32),
            shape((slots, packed_width), BF16),
            shape((total, LANES), F32),
        ],
        scratch_shapes=[
            pltpu.VMEM((SUBLANES, LANES), F32),
            pltpu.VMEM((total, half), F32),
            pltpu.VMEM((slots, LANES), F32),
        ],
        compiler_params=params(8),
        name="gradient",
    )(t_num, t_den, own_table, peer_table, table, there_table, part, peer_part, scaled, inverse)

    steps = 4
    step = width // steps
    grad_head = None

    def head_part(first, last, dep, so_far):
        extra = [dep] + ([] if so_far is None else [so_far])
        return pl.pallas_call(
            head_kernel,
            grid=(last - first,),
            in_specs=[
                pl.BlockSpec((voc, total), lambda i: (0, 0)),
                pl.BlockSpec((total, step), lambda i: (0, first + i)),
            ]
            + [anywhere()] * len(extra),
            out_specs=pl.BlockSpec((voc, step), lambda i: (0, first + i)),
            out_shape=shape((voc, width), BF16),
            input_output_aliases={} if so_far is None else {3: 0},
            compiler_params=params(12),
            cost_estimate=cost(2 * voc * step * (last - first)),
            name="head_grad",
        )(dlogits, normed, *extra)

    dlogits, normed = pl.pallas_call(
        dlogits_kernel,
        in_specs=[vmem()] * 5 + [anywhere()],
        out_specs=[vmem()] * 2,
        out_shape=[shape((voc, total), BF16), shape((total, width), BF16)],
        compiler_params=params(6),
        name="dlogits",
    )(targets, logits, meta, normed, normed_other, give)
    middle = 2
    grad_head = head_part(0, middle, give, None)
    sent = (own_part + swap(give, "ctx", blocks).astype(F32)).astype(BF16)
    for bit in inner_bits[:-2]:
        sent = sent + swap(sent, "ctx", bit)
    grad_head = head_part(middle, steps, sent, grad_head)
    loss_value = pl.pallas_call(
        loss_kernel,
        in_specs=[vmem(), anywhere()],
        out_specs=vmem(),
        out_shape=shape((1, 1), F32),
        compiler_params=params(4),
        name="loss",
    )(meta, sent)
    sent = join(sent, around(sent))
    other = swap(sent, "ctx", 1)

    def finish(side, part, *extra):
        chunks = 4
        return pl.pallas_call(
            lambda *refs: final_kernel(blocks, side, *refs),
            in_specs=[vmem()] * 6 + ([vmem(), anywhere()] if side else []),
            out_specs=[anywhere()] * (1 + side),
            out_shape=[shape((tok, width), BF16)] + ([shape((1, width), F32)] if side else []),
            input_output_aliases={7: 0} if side else {},
            scratch_shapes=[pltpu.VMEM((1, width), F32)] * side
            + [
                pltpu.VMEM((chunks, tok, half // chunks), BF16),
                pltpu.SemaphoreType.DMA((chunks + side,)),
            ],
            compiler_params=params(8),
            name="final",
        )(select, part, own, inverse, meta, gain_row, *extra)

    (grad_hidden,) = finish(0, sent)
    grad_hidden, grad_gain = finish(1, other, sent, grad_hidden)
    return (loss_value.reshape(()), grad_hidden, grad_head, grad_gain.reshape(width))


def solution(mesh):
    placed = (P("ctx", "vocab"), P("vocab"), P("ctx", "vocab"), P(), P(), P(), P())
    return jax.shard_map(
        device_step,
        mesh=mesh,
        in_specs=placed,
        out_specs=(P(), P("ctx", "vocab"), P("ctx", "vocab"), P("vocab")),
        check_vma=False,
    )
```
